32 devices in a mesh: tm: 4 (over y, x), lat: 8 (over z, core).
Axes of the slice: x: 2, y: 2, z: 4, core: 2. Of those that a mesh axis runs over, the one named last changes fastest.
Arguments:
- states: float32 [8, 69, 32, 256], P('tm', None, 'lat'), may hold values from -6 to 6
- observed: float32 [8, 69, 32, 256], P('tm', None, 'lat'), may hold values from -6 to 6
- conv_in: bfloat16 [3, 3, 256, 345], replicated, may hold values from -0.109375 to 0.109375
- bias_in: float32 [256], replicated, may hold values from -3 to 3
- conv_out: bfloat16 [3, 3, 69, 256], replicated, may hold values from -0.125 to 0.125
- bias_out: float32 [69], replicated, may hold values from -3 to 3
Outputs:
- scores: float32 [8, 69, 32, 256], P('tm', None, 'lat')
- guidance: float32 [8, 69, 32, 256], P('tm', None, 'lat')
The draws below stay inside these ranges and needn't reach their ends.
All inputs are finite; a program needn't handle non-finite values.
Results may differ from the reference program's by a relative error of at most 0.0045.
Values may be sent and summed in bfloat16 or wider, within the bound.
No kernel may reach another device: no remote copies, remote signals or barrier semaphores. Data moves between devices by JAX's collectives and lax.ppermute only.
A program may use at most 64 MiB of HBM per device.

```python
import jax
import jax.numpy as jnp
from jax import lax

C = 69
HID = 256
WINDOW = 5
LON = 256
NT = 8
NH = 32


def steps_of(stream_key, extent, cuts, smallest, high):
    def one(dim, shards_of):
        steps = jax.random.uniform(jax.random.fold_in(jax.random.fold_in(stream_key, 6), dim), (shards_of,), jnp.float32, smallest / len(cuts), high / len(cuts))
        return jnp.repeat(jnp.exp(steps), extent[dim] // shards_of).reshape((-1,) + (1,) * (len(extent) - dim - 1))

    loudness = one(*cuts[0])
    for cut in cuts[1:]:
        loudness = loudness * one(*cut)
    return loudness


def noise(key, dims, spread, bound, cuts=(), held_as=jnp.bfloat16):
    values = jax.random.normal(key, dims, jnp.float32) * spread
    if len(cuts) > 0:
        values = steps_of(key, dims, cuts, -0.22, 0.18) * values
    return jnp.clip(values, min=-bound, max=bound).astype(held_as)


def setup_inputs(seed: int = 0) -> dict:
    keys = jax.random.split(jax.random.key(seed), 7)
    states = noise(keys[0], (NT, C, NH, LON), 1.0, 6.0, ((0, 4), (2, 8)), jnp.float32)
    observed = noise(keys[1], (NT, C, NH, LON), 1.0, 6.0, ((0, 4), (2, 8)), jnp.float32)
    conv_in = noise(keys[2], (3, 3, HID, WINDOW * C), (9 * WINDOW * C) ** -0.5, 0.109375)
    bias_in = noise(keys[3], (HID,), 0.5, 3.0, (), jnp.float32)
    conv_out = noise(keys[4], (3, 3, C, HID), (9 * HID) ** -0.5, 0.125)
    bias_out = noise(keys[5], (C,), 0.5, 3.0, (), jnp.float32)
    return dict(states=states, observed=observed, conv_in=conv_in, bias_in=bias_in, conv_out=conv_out, bias_out=bias_out)


def convolve(padded, weights):
    rows = padded.shape[1] - 2
    channels = padded.shape[0]
    total = None
    for j in range(3):
        moved = jnp.roll(padded, 1 - j, axis=2)
        for i in range(3):
            band = moved[:, i:i + rows, :]
            term = jnp.dot(weights[i, j], band.reshape(channels, -1), preferred_element_type=jnp.float32)
            total = term if total is None else total + term
    return total.reshape(weights.shape[2], rows, padded.shape[2])


def pad_rows(field):
    return jnp.pad(field, ((0, 0), (1, 1), (0, 0)))


def flipped(weights):
    return jnp.transpose(weights[::-1, ::-1], (0, 1, 3, 2))


def silu_slope(value):
    sig = jax.nn.sigmoid(value)
    return sig * (1.0 + value * (1.0 - sig))


def reference(states, observed, conv_in, bias_in, conv_out, bias_out):
    total = states.shape[0]
    chans = states.shape[1]
    height = states.shape[2]
    width = states.shape[3]
    cast = states.astype(jnp.bfloat16)
    back_in = flipped(conv_in)
    back_out = flipped(conv_out)

    def one_window(index):
        picks = ((index + jnp.arange(WINDOW, dtype=jnp.int32) - 2) % total).astype(jnp.int32)
        stacked = jnp.take(cast, picks, axis=0).reshape(WINDOW * chans, height, width)
        pre = convolve(pad_rows(stacked), conv_in) + bias_in[:, None, None]
        act = jax.nn.silu(pre).astype(jnp.bfloat16)
        score = convolve(pad_rows(act), conv_out) + bias_out[:, None, None]
        target = lax.dynamic_index_in_dim(observed, index, 0, False)
        resid = (score - target).astype(jnp.bfloat16)
        grad_act = convolve(pad_rows(resid), back_out)
        grad_pre = (grad_act * silu_slope(pre)).astype(jnp.bfloat16)
        grad_window = convolve(pad_rows(grad_pre), back_in)
        return score, grad_window.reshape(WINDOW, chans, height, width)

    scores, grads = lax.map(one_window, jnp.arange(total, dtype=jnp.int32))
    guidance = jnp.roll(grads[:, 0], -2, axis=0)
    for k in range(1, WINDOW):
        guidance = guidance + jnp.roll(grads[:, k], k - 2, axis=0)
    return scores, guidance
```

```python
import functools

import jax
import jax.numpy as jnp
from jax import lax
from jax.experimental import pallas as pl
from jax.experimental.pallas import tpu as pltpu
from jax.sharding import PartitionSpec as P

F32 = jnp.float32
BF16 = jnp.bfloat16
LANES = 128
DEPTH = 4
REACH = 2
VMEM = pl.BlockSpec(memory_space=pltpu.VMEM)
SMEM = pl.BlockSpec(memory_space=pltpu.SMEM)


def up(value, step):
    return -(-value // step) * step


class Plan:
    def __init__(self, states, conv_in):
        self.n = lax.axis_size("tm")
        self.m = lax.axis_size("lat")
        self.local, self.chans, self.rows, self.lon = states.shape
        self.taps = conv_in.shape[0]
        self.hidden = conv_in.shape[2]
        self.window = conv_in.shape[3] // self.chans
        self.side = self.window // 2
        self.total = self.local * self.n
        self.wc = self.lon // self.n
        self.wx = self.wc + 2 * DEPTH
        self.wp = up(self.wx, 16)
        self.cp = up(self.chans, 8)
        self.packed = 2 * LANES
        self.pos = self.rows * self.local * self.wx
        self.posp = up(self.pos, LANES)
        self.half = REACH * self.local * self.wx
        self.cut = (self.pos - self.half) // LANES * LANES
        self.msg = max(self.posp - self.cut, up(self.half, LANES))
        self.cut = self.posp - self.msg
        self.shift = self.pos - self.half - self.cut
        self.out = self.rows * self.local * self.wc
        assert self.taps == 3 and LANES <= 2 * self.chans and 3 * self.chans <= self.packed
        assert self.out % LANES == 0 and LANES % self.wc == 0 and self.wx % 8 == 0
        assert self.lon % LANES == 0 and self.rows >= 2 * REACH and self.n & (self.n - 1) == 0

    def at(self, row, t):
        return (row * self.local + t) * self.wx


def call(kernel, outs, scratch, args, limit=48 << 20, name=None, cost=None):
    scalars = [SMEM if a.dtype == jnp.int32 else VMEM for a in args]
    return pl.pallas_call(
        kernel,
        out_shape=outs,
        in_specs=scalars,
        out_specs=[VMEM] * len(outs),
        scratch_shapes=scratch,
        compiler_params=pltpu.CompilerParams(vmem_limit_bytes=limit),
        name=name,
        cost_estimate=cost,
    )(*args)


def lanes_of(shape):
    return lax.broadcasted_iota(jnp.int32, shape, len(shape) - 1)


def split_kernel(p, where_ref, x_ref, *refs):
    outs, held = refs[: p.n], refs[p.n]
    me = where_ref[0]
    held[...] = jnp.zeros_like(held)
    for r in range(p.rows):
        for t in range(p.local):
            v = x_ref[t, r].astype(F32)
            start = p.at(r, t)
            base, off = start // LANES * LANES, start % LANES
            width = LANES if off + p.wx <= LANES else 2 * LANES
            lane = lanes_of((p.chans, width))
            inside = (lane >= off) & (lane < off + p.wx)
            for q in range(p.n):
                y = pltpu.roll(v, (off + DEPTH - p.wc * q) % p.lon, 1)[:, :width]
                old = held[q, : p.chans, base : base + width]
                held[q, : p.chans, base : base + width] = jnp.where(inside, y, old)
    for d in range(p.n):
        outs[d][...] = held[me ^ d].astype(outs[d].dtype)


def to_columns(block, rows_ref):
    depth, width = block.shape
    for m in range(width // LANES):
        tile = block[:, m * LANES : (m + 1) * LANES].astype(F32)
        tile = jnp.concatenate([tile, jnp.zeros((LANES - depth, LANES), F32)], axis=0)
        rows_ref[8 + m * LANES : 8 + (m + 1) * LANES, :] = tile.T


def taps_of(p, rows_ref, start, flip):
    v = [rows_ref[8 + start + j : 8 + start + j + p.wp, :] for j in (-1, 0, 1)]
    if flip:
        v = v[::-1]
    lane = lanes_of((p.wp, LANES))
    middle = pltpu.roll(v[1], p.chans, 1)
    low = jnp.where(lane < p.chans, v[0], middle)
    high = jnp.where(lane < 2 * p.chans - LANES, middle, pltpu.roll(v[2], 2 * p.chans - LANES, 1))
    return jnp.concatenate([low, high], axis=1).astype(BF16)


def untap(p, ref, lead, start, count, flip):
    before, after = (1, -1) if flip else (-1, 1)
    s = start
    first = ref[lead, s + before : s + before + count, :LANES]
    low = pltpu.roll(ref[lead, s : s + count, :LANES], LANES - p.chans, 1)
    high = pltpu.roll(ref[lead, s : s + count, LANES:], LANES - p.chans, 1)
    lane = lanes_of((count, LANES))
    middle = jnp.where(lane < LANES - p.chans, low, high)
    last = pltpu.roll(ref[lead, s + after : s + after + count, LANES:], 2 * LANES - 2 * p.chans, 1)
    return jnp.where(lane < p.chans, first + middle + last, 0.0)


def fill_taps(p, where_ref, blocks, near, far, rows_ref, taps_ref, flip, base):
    me, even = where_ref[0], where_ref[1] == 1
    for d in range(p.n):
        t0 = (me ^ d) * p.local + base
        to_columns(blocks[d][...], rows_ref)
        for r in range(p.rows):
            for t in range(p.local):
                taps_ref[REACH + r, t0 + t] = taps_of(p, rows_ref, p.at(r, t), flip)
        below = jnp.where(even, far[d], near[d])
        to_columns(below, rows_ref)
        for r in range(REACH):
            for t in range(p.local):
                taps_ref[r, t0 + t] = taps_of(p, rows_ref, p.shift + p.at(r, t), flip)
        above = jnp.where(even, near[d], far[d])
        to_columns(above, rows_ref)
        for r in range(REACH):
            for t in range(p.local):
                taps_ref[REACH + p.rows + r, t0 + t] = taps_of(p, rows_ref, p.at(r, t), flip)


def row_mask(p, where_ref, row):
    outside = ((row == 0) & (where_ref[2] == 1)) | ((row == p.rows + 1) & (where_ref[3] == 1))
    return jnp.where(outside, 0.0, 1.0)


def dot(a, b, transposed):
    dims = (((1,), (1 if transposed else 0,)), ((), ()))
    return lax.dot_general(a, b, dims, preferred_element_type=F32)


def forward_kernel(p, where_ref, *refs):
    n = p.n
    blocks, near, far, targets = refs[:n], refs[n], refs[n + 1], refs[n + 2 : 2 * n + 2]
    w_in, bias_in, w_out, bias_out = refs[2 * n + 2 : 2 * n + 6]
    slope_ref, own_ref = refs[2 * n + 6 : 2 * n + 8]
    scores = refs[2 * n + 8 : 3 * n + 7]
    resids = refs[3 * n + 7 : 4 * n + 7]
    rows_ref, taps_ref, act_ref, part_ref, wide_ref, thin_ref = refs[4 * n + 7 :]
    me = where_ref[0]
    flat = p.total * p.wp
    fill_taps(p, where_ref, blocks, near, far, rows_ref, taps_ref, False, p.side)
    for e in range(p.side):
        taps_ref[:, e] = taps_ref[:, p.total + e]
        taps_ref[:, p.total + p.side + e] = taps_ref[:, p.side + e]

    def hidden_row(row, carry):
        total = None
        for i in range(p.taps):
            for k in range(p.window):
                a = taps_ref[row + i, k : k + p.total].reshape(flat, p.packed)
                term = dot(a, w_in[i * p.window + k], True)
                total = term if total is None else total + term
        pre = total + bias_in[...]
        sig = 0.5 * jnp.tanh(0.5 * pre) + 0.5
        act = pre * sig
        slope = sig + act * (1.0 - sig)
        mask = row_mask(p, where_ref, row)
        act_ref[row] = (act * mask).astype(BF16).reshape(p.total, p.wp, p.hidden)
        slope_ref[row] = (slope * mask).reshape(p.total, p.wp, p.hidden)
        return carry

    lax.fori_loop(0, p.rows + 2, hidden_row, 0)
    wide_ref[...] = jnp.zeros_like(wide_ref)

    def score_row(row, carry):
        total = None
        for i in range(p.taps):
            term = dot(act_ref[row + i].reshape(flat, p.hidden), w_out[i], True)
            total = term if total is None else total + term
        part_ref[:, 8 : 8 + p.wp, :] = total.reshape(p.total, p.wp, p.packed)
        for d in range(n):
            for t in range(p.local):
                s = untap(p, part_ref, (me ^ d) * p.local + t, 8, p.wx, False) + bias_out[...]
                wide_ref[d, pl.ds(pl.multiple_of((row * p.local + t) * p.wx, 8), p.wx), :] = s
                thin_ref[d, pl.ds(pl.multiple_of((row * p.local + t) * p.wc, 8), p.wc), :] = s[DEPTH : DEPTH + p.wc]
        return carry

    lax.fori_loop(0, p.rows, score_row, 0)
    for d in range(n):
        for m in range(p.posp // LANES):
            cols = slice(m * LANES, (m + 1) * LANES)
            tile = wide_ref[d, cols, :].T[: p.cp]
            resids[d][:, cols] = (tile - targets[d][:, cols]).astype(BF16)
        for m in range(p.out // LANES):
            cols = slice(m * LANES, (m + 1) * LANES)
            tile = thin_ref[d, cols, :].T[: p.cp]
            if d == 0:
                own_ref[:, cols] = tile
            else:
                scores[d - 1][:, cols] = tile.astype(BF16)


def backward_kernel(p, where_ref, *refs):
    n = p.n
    blocks, near, far = refs[:n], refs[n], refs[n + 1]
    slope_ref, w_in, w_out, own_ref = refs[n + 2 : n + 6]
    outs = refs[n + 6 : 2 * n + 5]
    rows_ref, taps_ref, grad_ref, part_ref, thin_ref = refs[2 * n + 5 :]
    me = where_ref[0]
    flat = p.total * p.wp
    fill_taps(p, where_ref, blocks, near, far, rows_ref, taps_ref, True, 0)

    def hidden_row(row, carry):
        total = None
        for i in range(p.taps):
            a = taps_ref[row + 2 - i].reshape(flat, p.packed)
            term = dot(a, w_out[i], False)
            total = term if total is None else total + term
        grad = total.reshape(p.total, p.wp, p.hidden) * slope_ref[row]
        grad_ref[row, p.side : p.side + p.total] = grad.astype(BF16)
        return carry

    lax.fori_loop(0, p.rows + 2, hidden_row, 0)
    for e in range(p.side):
        grad_ref[:, e] = grad_ref[:, p.total + e]
        grad_ref[:, p.total + p.side + e] = grad_ref[:, p.side + e]

    def out_row(row, carry):
        total = None
        for i in range(p.taps):
            for k in range(p.window):
                shift = 2 * p.side - k
                a = grad_ref[row + 2 - i, shift : shift + p.total].reshape(flat, p.hidden)
                term = dot(a, w_in[i * p.window + k], False)
                total = term if total is None else total + term
        part_ref[:, 8 : 8 + p.wp, :] = total.reshape(p.total, p.wp, p.packed)
        for d in range(n):
            for t in range(p.local):
                g = untap(p, part_ref, (me ^ d) * p.local + t, 8 + DEPTH, p.wc, True)
                thin_ref[d, pl.ds(pl.multiple_of((row * p.local + t) * p.wc, 8), p.wc), :] = g
        return carry

    lax.fori_loop(0, p.rows, out_row, 0)
    for d in range(n):
        for m in range(p.out // LANES):
            cols = slice(m * LANES, (m + 1) * LANES)
            tile = thin_ref[d, cols, :].T[: p.cp]
            if d == 0:
                own_ref[:, cols] = tile
            else:
                outs[d - 1][:, cols] = tile.astype(BF16)


def join_kernel(p, where_ref, *refs):
    ins, out_ref, held = refs[: p.n], refs[p.n], refs[p.n + 1]
    me = where_ref[0]
    for d in range(p.n):
        held[me ^ d] = ins[d][...].astype(F32)
    per = LANES // p.wc
    for r in range(p.rows):
        for t in range(p.local):
            start = (r * p.local + t) * p.wc
            base, off = start // LANES * LANES, start % LANES
            for m in range(p.lon // LANES):
                tile = None
                for u in range(per):
                    piece = held[m * per + u, : p.chans, base : base + LANES]
                    step = (u * p.wc - off) % LANES
                    if step:
                        piece = pltpu.roll(piece, step, 1)
                    lane = lanes_of((p.chans, LANES))
                    tile = piece if tile is None else jnp.where(lane < u * p.wc, tile, piece)
                out_ref[t, r, :, m * LANES : (m + 1) * LANES] = tile


def send_tm(p, value, d):
    return lax.ppermute(value, "tm", [(i, i ^ d) for i in range(p.n)])


def send_lat(p, even, blocks):
    low = jnp.stack([b[:, : p.msg] for b in blocks])
    high = jnp.stack([b[:, p.cut :] for b in blocks])
    inner = [(i, i ^ 1) for i in range(p.m)]
    outer = [(i, ((i + 1) ^ 1) - 1) for i in range(1, p.m - 1)]
    far = lax.ppermute(jnp.where(even, low, high), "lat", outer)
    near = lax.ppermute(jnp.where(even, high, low), "lat", inner)
    return near, far


def shards(states, observed, conv_in, bias_in, conv_out, bias_out):
    p = Plan(states, conv_in)
    me, row = lax.axis_index("tm"), lax.axis_index("lat")
    even = row % 2 == 0
    where = jnp.stack([me, even.astype(jnp.int32), (row == 0).astype(jnp.int32), (row == p.m - 1).astype(jnp.int32)])
    where = where.astype(jnp.int32)
    sds = jax.ShapeDtypeStruct
    block = sds((p.cp, p.posp), BF16)
    thin = sds((p.cp, p.out), BF16)

    def split(field, dtype, name):
        turned = jnp.transpose(field.astype(dtype), (0, 2, 1, 3))
        scratch = [pltpu.VMEM((p.n, p.cp, p.posp), F32)]
        shape = [sds((p.cp, p.posp), dtype)] * p.n
        return call(functools.partial(split_kernel, p), shape, scratch, [where, turned], 8 << 20, name)

    mine = split(states, BF16, "split_states")
    theirs = [send_tm(p, mine[d], d) for d in range(1, p.n)]
    goal = split(observed, F32, "split_observed")
    goals = [goal[0]] + [send_tm(p, goal[d], d) for d in range(1, p.n)]
    blocks = [mine[0]] + theirs
    w_in = conv_in.reshape(p.taps, p.taps, p.hidden, p.window, p.chans)
    w_in = jnp.transpose(w_in, (0, 3, 2, 1, 4)).reshape(p.taps * p.window, p.hidden, p.taps * p.chans)
    w_in = jnp.pad(w_in, ((0, 0), (0, 0), (0, p.packed - p.taps * p.chans)))
    w_out = conv_out.reshape(p.taps, p.taps * p.chans, p.hidden)
    w_out = jnp.pad(w_out, ((0, 0), (0, p.packed - p.taps * p.chans), (0, 0)))
    b_in = bias_in.reshape(1, p.hidden)
    b_out = jnp.pad(bias_out, (0, LANES - p.chans)).reshape(1, LANES)
    near, far = send_lat(p, even, blocks)

    columns = pltpu.VMEM((p.posp + 32, LANES), F32)
    part = pltpu.VMEM((p.total, p.wp + 16, p.packed), F32)
    thin_rows = pltpu.VMEM((p.n, p.out, LANES), F32)
    deep = p.rows + 2 * REACH
    out = call(
        functools.partial(forward_kernel, p),
        [sds((p.rows + 2, p.total, p.wp, p.hidden), F32), sds((p.cp, p.out), F32)]
        + [thin] * (p.n - 1) + [block] * p.n,
        [
            columns,
            pltpu.VMEM((deep, p.total + 2 * p.side, p.wp, p.packed), BF16),
            pltpu.VMEM((p.rows + 2, p.total, p.wp, p.hidden), BF16),
            part,
            pltpu.VMEM((p.n, p.posp, LANES), F32),
            thin_rows,
        ],
        [where, *blocks, near, far, *goals, w_in, b_in, w_out, b_out],
        name="forward",
    )
    slope, own_scores, away, resids = out[0], out[1], out[2 : p.n + 1], out[p.n + 1 :]
    near, far = send_lat(p, even, resids)
    back = [own_scores] + [send_tm(p, away[d - 1], d) for d in range(1, p.n)]
    out = call(
        functools.partial(backward_kernel, p),
        [sds((p.cp, p.out), F32)] + [thin] * (p.n - 1),
        [
            columns,
            pltpu.VMEM((deep, p.total, p.wp, p.packed), BF16),
            pltpu.VMEM((p.rows + 2, p.total + 2 * p.side, p.wp, p.hidden), BF16),
            part,
            thin_rows,
        ],
        [where, *resids, near, far, slope, w_in, w_out],
        name="backward",
    )
    grads = [out[0]] + [send_tm(p, out[d], d) for d in range(1, p.n)]

    def join(parts, name):
        scratch = [pltpu.VMEM((p.n, p.cp, p.out), F32)]
        shape = [sds((p.local, p.rows, p.chans, p.lon), F32)]
        joined = call(functools.partial(join_kernel, p), shape, scratch, [where, *parts], 8 << 20, name)[0]
        return jnp.transpose(joined, (0, 2, 1, 3))

    return join(back, "join_scores"), join(grads, "join_guidance")


def solution(mesh):
    in_specs = (P("tm", None, "lat", None), P("tm", None, "lat", None), P(), P(), P(), P())
    out_specs = (P("tm", None, "lat", None), P("tm", None, "lat", None))
    return jax.shard_map(shards, mesh=mesh, in_specs=in_specs, out_specs=out_specs, check_vma=False)
```

```python
import functools

import jax
import jax.numpy as jnp
from jax import lax
from jax.experimental import pallas as pl
from jax.experimental.pallas import tpu as pltpu
from jax.sharding import PartitionSpec as P


F32 = jnp.float32
BF16 = jnp.bfloat16
LANES = 128
DEPTH = 4
REACH = 2
VMEM = pl.BlockSpec(memory_space=pltpu.VMEM)
SMEM = pl.BlockSpec(memory_space=pltpu.SMEM)


def up(value, step):
    return -(-value // step) * step


class Plan:
    def __init__(self, states, conv_in):
        self.n = lax.axis_size("tm")
        self.m = lax.axis_size("lat")
        self.local, self.chans, self.rows, self.lon = states.shape
        self.taps = conv_in.shape[0]
        self.hidden = conv_in.shape[2]
        self.window = conv_in.shape[3] // self.chans
        self.side = self.window // 2
        self.total = self.local * self.n
        self.wc = self.lon // self.n
        self.wx = self.wc + 2 * DEPTH
        self.wp = up(self.wx, 16)
        self.cp = up(self.chans, 8)
        self.packed = 2 * LANES
        self.pos = self.rows * self.local * self.wx
        self.posp = up(self.pos, LANES)
        self.half = REACH * self.local * self.wx
        self.cut = (self.pos - self.half) // LANES * LANES
        self.msg = max(self.posp - self.cut, up(self.half, LANES))
        self.cut = self.posp - self.msg
        self.shift = self.pos - self.half - self.cut
        self.out = self.rows * self.local * self.wc
        assert self.taps == 3 and LANES <= 2 * self.chans and 3 * self.chans <= self.packed
        assert self.out % LANES == 0 and LANES % self.wc == 0 and self.wx % 8 == 0
        assert self.lon % LANES == 0 and self.rows >= 2 * REACH and self.n & (self.n - 1) == 0

    def at(self, row, t):
        return (row * self.local + t) * self.wx


def call(kernel, outs, scratch, args, limit, microseconds, aliases={}):
    return pl.pallas_call(
        kernel,
        out_shape=outs,
        in_specs=[SMEM if a.dtype == jnp.int32 else VMEM for a in args],
        out_specs=[VMEM] * len(outs),
        scratch_shapes=scratch,
        input_output_aliases=aliases,
        compiler_params=pltpu.CompilerParams(vmem_limit_bytes=limit),
        cost_estimate=pl.CostEstimate(flops=int(microseconds * 1e9), bytes_accessed=0, transcendentals=0),
    )(*args)


def lanes_of(shape):
    return lax.broadcasted_iota(jnp.int32, shape, len(shape) - 1)


def split_kernel(p, where_ref, x_ref, *refs):
    outs, held = refs[: p.n], refs[p.n]
    me = where_ref[0]
    held[...] = jnp.zeros_like(held)
    for r in range(p.rows):
        for t in range(p.local):
            v = x_ref[t, :, r, :]
            start = p.at(r, t)
            base, off = start // LANES * LANES, start % LANES
            width = LANES if off + p.wx <= LANES else 2 * LANES
            lane = lanes_of((p.chans, width))
            inside = (lane >= off) & (lane < off + p.wx)
            for q in range(p.n):
                y = pltpu.roll(v, (off + DEPTH - p.wc * q) % p.lon, 1)[:, :width]
                old = held[q, : p.chans, base : base + width]
                held[q, : p.chans, base : base + width] = jnp.where(inside, y, old)
    for d in range(p.n):
        outs[d][...] = held[me ^ d].astype(outs[d].dtype)


def weights_kernel(p, k_in, k_out, w_in, w_out, flat_ref, held):
    held[...] = jnp.zeros_like(held)
    c = p.chans
    for i in range(p.taps):
        for j in range(p.taps):
            flat_ref[j, : p.window * c] = k_in[i, j].astype(F32)
        for k in range(p.window):
            for j in range(p.taps):
                held[k, j * c : (j + 1) * c, :] = flat_ref[j, k * c : (k + 1) * c, :]
            w_in[i * p.window + k] = held[k].astype(BF16)
        for j in range(p.taps):
            held[p.window, j * c : (j + 1) * c, :] = k_out[i, j].astype(F32)
        w_out[i] = held[p.window].astype(BF16)


def to_columns(block, rows_ref):
    depth, width = block.shape
    for m in range(width // LANES):
        tile = block[:, m * LANES : (m + 1) * LANES].astype(F32)
        tile = jnp.concatenate([tile, jnp.zeros((LANES - depth, LANES), F32)], axis=0)
        rows_ref[8 + m * LANES : 8 + (m + 1) * LANES, :] = tile.T


def taps_of(p, rows_ref, start, flip):
    v = [rows_ref[8 + start + j : 8 + start + j + p.wp, :] for j in (-1, 0, 1)]
    if flip:
        v = v[::-1]
    lane = lanes_of((p.wp, LANES))
    middle = pltpu.roll(v[1], p.chans, 1)
    low = jnp.where(lane < p.chans, v[0], middle)
    high = jnp.where(lane < 2 * p.chans - LANES, middle, pltpu.roll(v[2], 2 * p.chans - LANES, 1))
    return jnp.concatenate([low, high], axis=1).astype(BF16)


def untap(p, ref, lead, start, count, flip):
    before, after = (1, -1) if flip else (-1, 1)
    s = start
    first = ref[lead, s + before : s + before + count, :LANES]
    low = pltpu.roll(ref[lead, s : s + count, :LANES], LANES - p.chans, 1)
    high = pltpu.roll(ref[lead, s : s + count, LANES:], LANES - p.chans, 1)
    lane = lanes_of((count, LANES))
    middle = jnp.where(lane < LANES - p.chans, low, high)
    last = pltpu.roll(ref[lead, s + after : s + after + count, LANES:], 2 * LANES - 2 * p.chans, 1)
    return jnp.where(lane < p.chans, first + middle + last, 0.0)


def fill_own(p, where_ref, blocks, rows_ref, taps_ref, flip, base):
    me = where_ref[0]
    for d in range(p.n):
        t0 = (me ^ d) * p.local + base
        to_columns(blocks[d][...], rows_ref)
        for r in range(p.rows):
            for t in range(p.local):
                taps_ref[REACH + r, t0 + t] = taps_of(p, rows_ref, p.at(r, t), flip)


def fill_halo(p, where_ref, near, far, rows_ref, taps_ref, flip, base):
    me, even = where_ref[0], where_ref[1] == 1
    for d in range(p.n):
        t0 = (me ^ d) * p.local + base
        to_columns(jnp.where(even, far[d], near[d]), rows_ref)
        for r in range(REACH):
            for t in range(p.local):
                taps_ref[r, t0 + t] = taps_of(p, rows_ref, p.shift + p.at(r, t), flip)
        to_columns(jnp.where(even, near[d], far[d]), rows_ref)
        for r in range(REACH):
            for t in range(p.local):
                taps_ref[REACH + p.rows + r, t0 + t] = taps_of(p, rows_ref, p.at(r, t), flip)


def wrap(p, ref, begin, count):
    for row in range(begin, begin + count):
        for e in range(p.side):
            ref[row, e] = ref[row, p.total + e]
            ref[row, p.total + p.side + e] = ref[row, p.side + e]


def row_mask(p, where_ref, row):
    outside = ((row == 0) & (where_ref[2] == 1)) | ((row == p.rows + 1) & (where_ref[3] == 1))
    return jnp.where(outside, 0.0, 1.0)


def dot(a, b, transposed):
    dims = (((1,), (1 if transposed else 0,)), ((), ()))
    return lax.dot_general(a, b, dims, preferred_element_type=F32)


def hidden_rows(p, where_ref, taps_ref, w_in, bias_in, act_ref, slope_ref, count, row_of):
    def body(step, carry):
        row = row_of(step)
        total = None
        for i in range(p.taps):
            for k in range(p.window):
                a = taps_ref[row + i, k : k + p.total].reshape(p.total * p.wp, p.packed)
                term = dot(a, w_in[i * p.window + k], False)
                total = term if total is None else total + term
        pre = total + bias_in[...]
        sig = 0.5 * jnp.tanh(0.5 * pre) + 0.5
        act = pre * sig
        slope = sig + act * (1.0 - sig)
        mask = row_mask(p, where_ref, row)
        act_ref[row] = (act * mask).astype(BF16).reshape(p.total, p.wp, p.hidden)
        slope_ref[row] = (slope * mask).reshape(p.total, p.wp, p.hidden)
        return carry

    lax.fori_loop(0, count, body, 0)


def inner_kernel(p, where_ref, *refs):
    blocks, w_in, bias_in = refs[: p.n], refs[p.n], refs[p.n + 1]
    taps_ref, act_ref, slope_ref, rows_ref = refs[p.n + 2 :]
    fill_own(p, where_ref, blocks, rows_ref, taps_ref, False, p.side)
    wrap(p, taps_ref, REACH, p.rows)
    hidden_rows(p, where_ref, taps_ref, w_in, bias_in, act_ref, slope_ref, p.rows - 2, lambda s: s + REACH)


def score_kernel(p, where_ref, *refs):
    n = p.n
    near, far, targets = refs[0], refs[1], refs[2 : n + 2]
    w_in, bias_in, w_out, bias_out = refs[n + 2 : n + 6]
    refs = refs[n + 9 :]
    taps_ref, act_ref, slope_ref, wide_ref = refs[:4]
    resids = refs[4 : n + 4]
    rows_ref, part_ref = refs[n + 4 :]
    me = where_ref[0]
    fill_halo(p, where_ref, near, far, rows_ref, taps_ref, False, p.side)
    wrap(p, taps_ref, 0, REACH)
    wrap(p, taps_ref, REACH + p.rows, REACH)
    edge = lambda s: jnp.where(s < REACH, s, s + p.rows - 2)
    hidden_rows(p, where_ref, taps_ref, w_in, bias_in, act_ref, slope_ref, 2 * REACH, edge)
    wide_ref[...] = jnp.zeros_like(wide_ref)

    def score_row(row, carry):
        total = None
        for i in range(p.taps):
            term = dot(act_ref[row + i].reshape(p.total * p.wp, p.hidden), w_out[i], True)
            total = term if total is None else total + term
        part_ref[:, 8 : 8 + p.wp, :] = total.reshape(p.total, p.wp, p.packed)
        for d in range(n):
            for t in range(p.local):
                s = untap(p, part_ref, (me ^ d) * p.local + t, 8, p.wx, False) + bias_out[...]
                wide_ref[d, pl.ds(pl.multiple_of((row * p.local + t) * p.wx, 8), p.wx), :] = s
        return carry

    lax.fori_loop(0, p.rows, score_row, 0)
    for d in range(n):
        for m in range(p.posp // LANES):
            cols = slice(m * LANES, (m + 1) * LANES)
            tile = wide_ref[d, cols, :].T[: p.cp]
            resids[d][:, cols] = (tile - targets[d][:, cols]).astype(BF16)


def gradient_rows(p, taps_ref, w_out, slope_ref, grad_ref, count, row_of):
    def body(step, carry):
        row = row_of(step)
        total = None
        for i in range(p.taps):
            a = taps_ref[row + 2 - i].reshape(p.total * p.wp, p.packed)
            term = dot(a, w_out[i], False)
            total = term if total is None else total + term
        grad = total.reshape(p.total, p.wp, p.hidden) * slope_ref[row]
        grad_ref[row, p.side : p.side + p.total] = grad.astype(BF16)
        return carry

    lax.fori_loop(0, count, body, 0)


def back_inner_kernel(p, where_ref, *refs):
    n = p.n
    blocks, slope_ref, w_out, wide_ref = refs[:n], refs[n], refs[n + 1], refs[n + 2]
    taps_ref, grad_ref = refs[n + 3 : n + 5]
    own_ref, scores = refs[n + 5], refs[n + 6 : 2 * n + 5]
    rows_ref, thin_ref = refs[2 * n + 5 :]
    fill_own(p, where_ref, blocks, rows_ref, taps_ref, True, 0)
    gradient_rows(p, taps_ref, w_out, slope_ref, grad_ref, p.rows - 2, lambda s: s + REACH)
    wrap(p, grad_ref, REACH, p.rows - 2)
    for d in range(n):
        for r in range(p.rows):
            for t in range(p.local):
                start = p.at(r, t) + DEPTH
                at = (r * p.local + t) * p.wc
                thin_ref[at : at + p.wc, :] = wide_ref[d, start : start + p.wc, :]
        turn(p, thin_ref, own_ref if d == 0 else scores[d - 1], 0)


def turn(p, thin_ref, out_ref, begin):
    for m in range(p.out // LANES):
        tile = thin_ref[m * LANES : (m + 1) * LANES, :].T[: p.cp]
        out_ref[:, begin + m * LANES : begin + (m + 1) * LANES] = tile.astype(out_ref.dtype)


def back_outer_kernel(p, where_ref, near, far, slope_ref, w_out, _taps, _grad, taps_ref, grad_ref, rows_ref):
    fill_halo(p, where_ref, near, far, rows_ref, taps_ref, True, 0)
    edge = lambda s: jnp.where(s < REACH, s, s + p.rows - 2)
    gradient_rows(p, taps_ref, w_out, slope_ref, grad_ref, 2 * REACH, edge)
    wrap(p, grad_ref, 0, REACH)
    wrap(p, grad_ref, p.rows, REACH)


def guide_kernel(p, d, where_ref, grad_ref, w_in, scores_ref, out_ref, part_ref, thin_ref):
    t0 = (where_ref[0] ^ d) * p.local
    total = None
    for i in range(p.taps):
        for k in range(p.window):
            a = grad_ref[2 - i : 2 - i + p.rows, pl.ds(t0 + 2 * p.side - k, p.local)]
            a = a.reshape(p.rows * p.local * p.wp, p.hidden)
            term = dot(a, w_in[i * p.window + k], True)
            total = term if total is None else total + term
    part_ref[:, 8 : 8 + p.wp, :] = total.reshape(p.rows * p.local, p.wp, p.packed)
    for r in range(p.rows * p.local):
        thin_ref[r * p.wc : (r + 1) * p.wc, :] = untap(p, part_ref, r, 8 + DEPTH, p.wc, True)
    out_ref[:, : p.out] = scores_ref[...]
    turn(p, thin_ref, out_ref, p.out)


def join_kernel(p, where_ref, *refs):
    ins, outs, held = refs[: p.n], refs[p.n : p.n + 2], refs[p.n + 2]
    me = where_ref[0]
    for d in range(p.n):
        held[me ^ d] = ins[d][...].astype(F32)
    per = LANES // p.wc
    lane = lanes_of((p.chans, LANES))
    for which in range(2):
        for r in range(p.rows):
            for t in range(p.local):
                start = which * p.out + (r * p.local + t) * p.wc
                base, off = start // LANES * LANES, start % LANES
                for m in range(p.lon // LANES):
                    tile = None
                    for u in range(per):
                        piece = held[m * per + u, : p.chans, base : base + LANES]
                        step = (u * p.wc - off) % LANES
                        if step:
                            piece = pltpu.roll(piece, step, 1)
                        tile = piece if tile is None else jnp.where(lane < u * p.wc, tile, piece)
                    outs[which][t, :, r, m * LANES : (m + 1) * LANES] = tile


def send_tm(p, value, d):
    return lax.ppermute(value, "tm", [(i, i ^ d) for i in range(p.n)])


def send_lat(p, even, blocks):
    low = jnp.stack([b[:, : p.msg] for b in blocks])
    high = jnp.stack([b[:, p.cut :] for b in blocks])
    inner = [(i, i ^ 1) for i in range(p.m)]
    outer = [(i, ((i + 1) ^ 1) - 1) for i in range(1, p.m - 1)]
    far = lax.ppermute(jnp.where(even, low, high), "lat", outer)
    near = lax.ppermute(jnp.where(even, high, low), "lat", inner)
    return near, far


def shards(states, observed, conv_in, bias_in, conv_out, bias_out):
    p = Plan(states, conv_in)
    n = p.n
    me, row = lax.axis_index("tm"), lax.axis_index("lat")
    even = row % 2 == 0
    where = jnp.stack([me, even.astype(jnp.int32), (row == 0).astype(jnp.int32), (row == p.m - 1).astype(jnp.int32)])
    where = where.astype(jnp.int32)
    sds = jax.ShapeDtypeStruct
    kernel = functools.partial
    scratch = pltpu.VMEM

    def split(field, dtype):
        shape = [sds((p.cp, p.posp), dtype)] * n
        held = [scratch((n, p.cp, p.posp), F32)]
        return call(kernel(split_kernel, p), shape, held, [where, field], 8 << 20, 1.5)

    mine = split(states, BF16)
    blocks = [mine[0]] + [send_tm(p, mine[d], d) for d in range(1, n)]
    w_in, w_out = call(
        kernel(weights_kernel, p),
        [sds((p.taps * p.window, p.packed, p.hidden), BF16), sds((p.taps, p.packed, p.hidden), BF16)],
        [scratch((p.taps, up(p.window * p.chans, 8), p.hidden), F32), scratch((p.window + 1, p.packed, p.hidden), F32)],
        [jnp.swapaxes(conv_in, 2, 3), conv_out],
        16 << 20, 2,
    )
    goal = split(observed, F32)
    goals = [goal[0]] + [send_tm(p, goal[d], d) for d in range(1, n)]
    b_in = bias_in.reshape(1, p.hidden)
    b_out = jnp.pad(bias_out, (0, LANES - p.chans)).reshape(1, LANES)
    near, far = send_lat(p, even, blocks)

    columns = scratch((p.posp + 32, LANES), F32)
    deep = p.rows + 2 * REACH
    around = p.total + 2 * p.side
    taps_shape = sds((deep, around, p.wp, p.packed), BF16)
    act_shape = sds((p.rows + 2, p.total, p.wp, p.hidden), BF16)
    slope_shape = sds((p.rows + 2, p.total, p.wp, p.hidden), F32)
    inner = call(
        kernel(inner_kernel, p), [taps_shape, act_shape, slope_shape], [columns],
        [where, *blocks, w_in, b_in], 24 << 20, 6,
    )
    part = scratch((p.total, p.wp + 16, p.packed), F32)
    out = call(
        kernel(score_kernel, p),
        [taps_shape, act_shape, slope_shape, sds((n, p.posp, LANES), F32)] + [sds((p.cp, p.posp), BF16)] * n,
        [columns, part],
        [where, near, far, *goals, w_in, b_in, w_out, b_out, *inner],
        32 << 20, 12, {n + 7: 0, n + 8: 1, n + 9: 2},
    )
    slope, wide, resids = out[2], out[3], out[4:]
    near, far = send_lat(p, even, resids)
    taps_shape = sds((deep, p.total, p.wp, p.packed), BF16)
    grad_shape = sds((p.rows + 2, around, p.wp, p.hidden), BF16)
    thin_rows = scratch((p.out, LANES), F32)
    out = call(
        kernel(back_inner_kernel, p),
        [taps_shape, grad_shape, sds((p.cp, p.out), F32)] + [sds((p.cp, p.out), BF16)] * (n - 1),
        [columns, thin_rows],
        [where, *resids, slope, w_out, wide], 24 << 20, 4,
    )
    taps, grad, scores = out[0], out[1], out[2:]
    taps, grad = call(
        kernel(back_outer_kernel, p), [taps_shape, grad_shape], [columns],
        [where, near, far, slope, w_out, taps, grad], 24 << 20, 3, {5: 0, 6: 1},
    )
    parts = [None] * n
    for d in [*range(n - 1, 0, -1), 0]:
        part = scratch((p.rows * p.local, p.wp + 16, p.packed), F32)
        parts[d] = call(
            kernel(guide_kernel, p, d), [sds((p.cp, 2 * p.out), scores[d].dtype)], [part, thin_rows],
            [where, grad, w_in, scores[d]], 16 << 20, 2,
        )[0]
        if d:
            parts[d] = send_tm(p, parts[d], d)
    shape = [sds((p.local, p.chans, p.rows, p.lon), F32)] * 2
    held = [scratch((n, p.cp, 2 * p.out), F32)]
    return tuple(call(kernel(join_kernel, p), shape, held, [where, *parts], 16 << 20, 1.5))


def solution(mesh):
    in_specs = (P("tm", None, "lat", None), P("tm", None, "lat", None), P(), P(), P(), P())
    out_specs = (P("tm", None, "lat", None), P("tm", None, "lat", None))
    return jax.shard_map(shards, mesh=mesh, in_specs=in_specs, out_specs=out_specs, check_vma=False)
```

```python
import functools

import jax
import jax.numpy as jnp
from jax import lax
from jax.experimental import pallas as pl
from jax.experimental.pallas import tpu as pltpu
from jax.sharding import PartitionSpec as P


F32 = jnp.float32
BF16 = jnp.bfloat16
LANES = 128
DEPTH = 4
REACH = 2
VMEM = pl.BlockSpec(memory_space=pltpu.VMEM)
SMEM = pl.BlockSpec(memory_space=pltpu.SMEM)


def up(value, step):
    return -(-value // step) * step


class Plan:
    def __init__(self, states, conv_in):
        self.n = lax.axis_size("tm")
        self.m = lax.axis_size("lat")
        self.local, self.chans, self.rows, self.lon = states.shape
        self.taps = conv_in.shape[0]
        self.hidden = conv_in.shape[2]
        self.window = conv_in.shape[3] // self.chans
        self.side = self.window // 2
        self.total = self.local * self.n
        self.wc = self.lon // self.n
        self.wx = self.wc + 2 * DEPTH
        self.wp = up(self.wx, 16)
        self.cp = up(self.chans, 8)
        self.packed = 2 * LANES
        self.pos = self.rows * self.local * self.wx
        self.posp = up(self.pos, LANES)
        self.half = REACH * self.local * self.wx
        self.cut = (self.pos - self.half) // LANES * LANES
        self.msg = max(self.posp - self.cut, up(self.half, LANES))
        self.cut = self.posp - self.msg
        self.shift = self.pos - self.half - self.cut
        self.out = self.rows * self.local * self.wc
        assert self.taps == 3 and LANES <= 2 * self.chans and 3 * self.chans <= self.packed
        assert self.out % LANES == 0 and LANES % self.wc == 0 and self.wx % 8 == 0
        assert self.lon % LANES == 0 and self.rows >= 2 * REACH and self.n & (self.n - 1) == 0

    def at(self, row, t):
        return (row * self.local + t) * self.wx


def call(kernel, outs, scratch, args, limit, microseconds, aliases={}):
    return pl.pallas_call(
        kernel,
        out_shape=outs,
        in_specs=[SMEM if a.dtype == jnp.int32 else VMEM for a in args],
        out_specs=[VMEM] * len(outs),
        scratch_shapes=scratch,
        input_output_aliases=aliases,
        compiler_params=pltpu.CompilerParams(vmem_limit_bytes=limit),
        cost_estimate=pl.CostEstimate(flops=int(microseconds * 1e9), bytes_accessed=0, transcendentals=0),
    )(*args)


def lanes_of(shape):
    return lax.broadcasted_iota(jnp.int32, shape, len(shape) - 1)


def split_kernel(p, where_ref, x_ref, *refs):
    outs, held = refs[: p.n], refs[p.n]
    me = where_ref[0]
    held[...] = jnp.zeros_like(held)
    for r in range(p.rows):
        for t in range(p.local):
            v = x_ref[t, :, r, :]
            start = p.at(r, t)
            base, off = start // LANES * LANES, start % LANES
            width = LANES if off + p.wx <= LANES else 2 * LANES
            lane = lanes_of((p.chans, width))
            inside = (lane >= off) & (lane < off + p.wx)
            for q in range(p.n):
                y = pltpu.roll(v, (off + DEPTH - p.wc * q) % p.lon, 1)[:, :width]
                old = held[q, : p.chans, base : base + width]
                held[q, : p.chans, base : base + width] = jnp.where(inside, y, old)
    for d in range(p.n):
        outs[d][...] = held[me ^ d].astype(outs[d].dtype)


def weights_kernel(p, k_in, k_out, w_in, w_out, flat_ref, held):
    held[...] = jnp.zeros_like(held)
    c = p.chans
    for i in range(p.taps):
        for j in range(p.taps):
            flat_ref[j, : p.window * c] = k_in[i, j].astype(F32)
        for k in range(p.window):
            for j in range(p.taps):
                held[k, j * c : (j + 1) * c, :] = flat_ref[j, k * c : (k + 1) * c, :]
            w_in[i * p.window + k] = held[k].astype(BF16)
        for j in range(p.taps):
            held[p.window, j * c : (j + 1) * c, :] = k_out[i, j].astype(F32)
        w_out[i] = held[p.window].astype(BF16)


def to_columns(block, rows_ref):
    depth, width = block.shape
    for m in range(width // LANES):
        tile = block[:, m * LANES : (m + 1) * LANES].astype(F32)
        tile = jnp.concatenate([tile, jnp.zeros((LANES - depth, LANES), F32)], axis=0)
        rows_ref[8 + m * LANES : 8 + (m + 1) * LANES, :] = tile.T


def taps_of(p, rows_ref, start, flip):
    v = [rows_ref[8 + start + j : 8 + start + j + p.wp, :] for j in (-1, 0, 1)]
    if flip:
        v = v[::-1]
    lane = lanes_of((p.wp, LANES))
    middle = pltpu.roll(v[1], p.chans, 1)
    low = jnp.where(lane < p.chans, v[0], middle)
    high = jnp.where(lane < 2 * p.chans - LANES, middle, pltpu.roll(v[2], 2 * p.chans - LANES, 1))
    return jnp.concatenate([low, high], axis=1).astype(BF16)


def untap(p, ref, lead, start, count, flip):
    before, after = (1, -1) if flip else (-1, 1)
    s = start
    first = ref[lead, s + before : s + before + count, :LANES]
    low = pltpu.roll(ref[lead, s : s + count, :LANES], LANES - p.chans, 1)
    high = pltpu.roll(ref[lead, s : s + count, LANES:], LANES - p.chans, 1)
    lane = lanes_of((count, LANES))
    middle = jnp.where(lane < LANES - p.chans, low, high)
    last = pltpu.roll(ref[lead, s + after : s + after + count, LANES:], 2 * LANES - 2 * p.chans, 1)
    return jnp.where(lane < p.chans, first + middle + last, 0.0)


def fill_own(p, where_ref, blocks, rows_ref, taps_ref, flip, base):
    me = where_ref[0]
    for d in range(p.n):
        t0 = (me ^ d) * p.local + base
        to_columns(blocks[d][...], rows_ref)
        for r in range(p.rows):
            for t in range(p.local):
                taps_ref[REACH + r, t0 + t] = taps_of(p, rows_ref, p.at(r, t), flip)


def fill_halo(p, where_ref, near, far, rows_ref, taps_ref, flip, base):
    me, even = where_ref[0], where_ref[1] == 1
    for d in range(p.n):
        t0 = (me ^ d) * p.local + base
        to_columns(jnp.where(even, far[d], near[d]), rows_ref)
        for r in range(REACH):
            for t in range(p.local):
                taps_ref[r, t0 + t] = taps_of(p, rows_ref, p.shift + p.at(r, t), flip)
        to_columns(jnp.where(even, near[d], far[d]), rows_ref)
        for r in range(REACH):
            for t in range(p.local):
                taps_ref[REACH + p.rows + r, t0 + t] = taps_of(p, rows_ref, p.at(r, t), flip)


def wrap(p, ref, begin, count):
    for row in range(begin, begin + count):
        for e in range(p.side):
            ref[row, e] = ref[row, p.total + e]
            ref[row, p.total + p.side + e] = ref[row, p.side + e]


def row_mask(p, where_ref, row):
    outside = ((row == 0) & (where_ref[2] == 1)) | ((row == p.rows + 1) & (where_ref[3] == 1))
    return jnp.where(outside, 0.0, 1.0)


def dot(a, b, transposed):
    dims = (((1,), (1 if transposed else 0,)), ((), ()))
    return lax.dot_general(a, b, dims, preferred_element_type=F32)


def hidden_rows(p, where_ref, taps_ref, w_in, bias_in, act_ref, slope_ref, count, row_of):
    def body(step, carry):
        row = row_of(step)
        total = None
        for i in range(p.taps):
            for k in range(p.window):
                a = taps_ref[row + i, k : k + p.total].reshape(p.total * p.wp, p.packed)
                term = dot(a, w_in[i * p.window + k], False)
                total = term if total is None else total + term
        pre = total + bias_in[...]
        sig = 0.5 * jnp.tanh(0.5 * pre) + 0.5
        act = pre * sig
        slope = sig + act * (1.0 - sig)
        mask = row_mask(p, where_ref, row)
        act_ref[row] = (act * mask).astype(BF16).reshape(p.total, p.wp, p.hidden)
        slope_ref[row] = (slope * mask).reshape(p.total, p.wp, p.hidden)
        return carry

    lax.fori_loop(0, count, body, 0)


def inner_kernel(p, where_ref, *refs):
    blocks, w_in, bias_in = refs[: p.n], refs[p.n], refs[p.n + 1]
    taps_ref, act_ref, slope_ref, rows_ref = refs[p.n + 2 :]
    fill_own(p, where_ref, blocks, rows_ref, taps_ref, False, p.side)
    wrap(p, taps_ref, REACH, p.rows)
    hidden_rows(p, where_ref, taps_ref, w_in, bias_in, act_ref, slope_ref, p.rows - 2, lambda s: s + REACH)


def outer_kernel(p, where_ref, near, far, w_in, bias_in, _taps, _act, _slope, taps_ref, act_ref, slope_ref, rows_ref):
    fill_halo(p, where_ref, near, far, rows_ref, taps_ref, False, p.side)
    wrap(p, taps_ref, 0, REACH)
    wrap(p, taps_ref, REACH + p.rows, REACH)
    edge = lambda s: jnp.where(s < REACH, s, s + p.rows - 2)
    hidden_rows(p, where_ref, taps_ref, w_in, bias_in, act_ref, slope_ref, 2 * REACH, edge)


def score_kernel(p, where_ref, *refs):
    n = p.n
    act_ref, w_out, bias_out = refs[:3]
    targets, wide_ref, resids, part_ref = refs[3 : n + 3], refs[n + 3], refs[n + 4 : 2 * n + 4], refs[2 * n + 4]
    me = where_ref[0]
    wide_ref[...] = jnp.zeros_like(wide_ref)

    def score_row(row, carry):
        total = None
        for i in range(p.taps):
            term = dot(act_ref[row + i].reshape(p.total * p.wp, p.hidden), w_out[i], True)
            total = term if total is None else total + term
        part_ref[:, 8 : 8 + p.wp, :] = total.reshape(p.total, p.wp, p.packed)
        for d in range(n):
            for t in range(p.local):
                s = untap(p, part_ref, (me ^ d) * p.local + t, 8, p.wx, False) + bias_out[...]
                wide_ref[d, pl.ds(pl.multiple_of((row * p.local + t) * p.wx, 8), p.wx), :] = s
        return carry

    lax.fori_loop(0, p.rows, score_row, 0)
    for d in range(n):
        for m in range(p.posp // LANES):
            cols = slice(m * LANES, (m + 1) * LANES)
            tile = wide_ref[d, cols, :].T[: p.cp]
            resids[d][:, cols] = (tile - targets[d][:, cols]).astype(BF16)


def gradient_rows(p, taps_ref, w_out, slope_ref, grad_ref, count, row_of):
    def body(step, carry):
        row = row_of(step)
        total = None
        for i in range(p.taps):
            a = taps_ref[row + 2 - i].reshape(p.total * p.wp, p.packed)
            term = dot(a, w_out[i], False)
            total = term if total is None else total + term
        grad = total.reshape(p.total, p.wp, p.hidden) * slope_ref[row]
        grad_ref[row, p.side : p.side + p.total] = grad.astype(BF16)
        return carry

    lax.fori_loop(0, count, body, 0)


def back_inner_kernel(p, where_ref, *refs):
    n = p.n
    blocks, slope_ref, w_out, wide_ref = refs[:n], refs[n], refs[n + 1], refs[n + 2]
    taps_ref, grad_ref = refs[n + 3 : n + 5]
    own_ref, scores = refs[n + 5], refs[n + 6 : 2 * n + 5]
    rows_ref, thin_ref = refs[2 * n + 5 :]
    fill_own(p, where_ref, blocks, rows_ref, taps_ref, True, 0)
    gradient_rows(p, taps_ref, w_out, slope_ref, grad_ref, p.rows - 2, lambda s: s + REACH)
    wrap(p, grad_ref, REACH, p.rows - 2)
    for d in range(n):
        for r in range(p.rows):
            for t in range(p.local):
                start = p.at(r, t) + DEPTH
                at = (r * p.local + t) * p.wc
                thin_ref[at : at + p.wc, :] = wide_ref[d, start : start + p.wc, :]
        turn(p, thin_ref, own_ref if d == 0 else scores[d - 1], 0)


def turn(p, thin_ref, out_ref, begin):
    for m in range(p.out // LANES):
        tile = thin_ref[m * LANES : (m + 1) * LANES, :].T[: p.cp]
        out_ref[:, begin + m * LANES : begin + (m + 1) * LANES] = tile.astype(out_ref.dtype)


def back_outer_kernel(p, where_ref, near, far, slope_ref, w_out, _taps, _grad, taps_ref, grad_ref, rows_ref):
    fill_halo(p, where_ref, near, far, rows_ref, taps_ref, True, 0)
    edge = lambda s: jnp.where(s < REACH, s, s + p.rows - 2)
    gradient_rows(p, taps_ref, w_out, slope_ref, grad_ref, 2 * REACH, edge)
    wrap(p, grad_ref, 0, REACH)
    wrap(p, grad_ref, p.rows, REACH)


def guide_kernel(p, d, where_ref, grad_ref, w_in, scores_ref, out_ref, part_ref, thin_ref):
    t0 = (where_ref[0] ^ d) * p.local
    total = None
    for i in range(p.taps):
        for k in range(p.window):
            a = grad_ref[2 - i : 2 - i + p.rows, pl.ds(t0 + 2 * p.side - k, p.local)]
            a = a.reshape(p.rows * p.local * p.wp, p.hidden)
            term = dot(a, w_in[i * p.window + k], True)
            total = term if total is None else total + term
    part_ref[:, 8 : 8 + p.wp, :] = total.reshape(p.rows * p.local, p.wp, p.packed)
    for r in range(p.rows * p.local):
        thin_ref[r * p.wc : (r + 1) * p.wc, :] = untap(p, part_ref, r, 8 + DEPTH, p.wc, True)
    out_ref[:, : p.out] = scores_ref[...]
    turn(p, thin_ref, out_ref, p.out)


def join_kernel(p, where_ref, *refs):
    ins, outs, held = refs[: p.n], refs[p.n : p.n + 2], refs[p.n + 2]
    me = where_ref[0]
    for d in range(p.n):
        held[me ^ d] = ins[d][...].astype(F32)
    per = LANES // p.wc
    lane = lanes_of((p.chans, LANES))
    for which in range(2):
        for r in range(p.rows):
            for t in range(p.local):
                start = which * p.out + (r * p.local + t) * p.wc
                base, off = start // LANES * LANES, start % LANES
                for m in range(p.lon // LANES):
                    tile = None
                    for u in range(per):
                        piece = held[m * per + u, : p.chans, base : base + LANES]
                        step = (u * p.wc - off) % LANES
                        if step:
                            piece = pltpu.roll(piece, step, 1)
                        tile = piece if tile is None else jnp.where(lane < u * p.wc, tile, piece)
                    outs[which][t, :, r, m * LANES : (m + 1) * LANES] = tile


def send_tm(p, value, d):
    return lax.ppermute(value, "tm", [(i, i ^ d) for i in range(p.n)])


def relay_tm(p, blocks, bit):
    moving = [d for d in range(p.n) if d & bit]
    moved = send_tm(p, jnp.stack([blocks[d] for d in moving]), bit)
    blocks = list(blocks)
    for at, d in enumerate(moving):
        blocks[d] = moved[at]
    return blocks


def send_lat(p, even, blocks):
    low = jnp.stack([b[:, : p.msg] for b in blocks])
    high = jnp.stack([b[:, p.cut :] for b in blocks])
    inner = [(i, i ^ 1) for i in range(p.m)]
    outer = [(i, ((i + 1) ^ 1) - 1) for i in range(1, p.m - 1)]
    near = lax.ppermute(jnp.where(even, high, low), "lat", inner)
    far = lax.ppermute(jnp.where(even, low, high), "lat", outer)
    return near, far


def shards(states, observed, conv_in, bias_in, conv_out, bias_out):
    p = Plan(states, conv_in)
    n = p.n
    me, row = lax.axis_index("tm"), lax.axis_index("lat")
    even = row % 2 == 0
    where = jnp.stack([me, even.astype(jnp.int32), (row == 0).astype(jnp.int32), (row == p.m - 1).astype(jnp.int32)])
    where = where.astype(jnp.int32)
    sds = jax.ShapeDtypeStruct
    kernel = functools.partial
    scratch = pltpu.VMEM

    def split(field, dtype):
        shape = [sds((p.cp, p.posp), dtype)] * n
        held = [scratch((n, p.cp, p.posp), F32)]
        return call(kernel(split_kernel, p), shape, held, [where, field], 8 << 20, 1.5)

    mine = split(states, BF16)
    blocks = [mine[0]] + [send_tm(p, mine[d], d) for d in range(1, n)]
    w_in, w_out = call(
        kernel(weights_kernel, p),
        [sds((p.taps * p.window, p.packed, p.hidden), BF16), sds((p.taps, p.packed, p.hidden), BF16)],
        [scratch((p.taps, up(p.window * p.chans, 8), p.hidden), F32), scratch((p.window + 1, p.packed, p.hidden), F32)],
        [jnp.swapaxes(conv_in, 2, 3), conv_out],
        16 << 20, 2,
    )
    goal = split(observed, F32)
    stages = [1 << b for b in range(n.bit_length() - 1)]
    goals = relay_tm(p, goal, stages[0])
    b_in = bias_in.reshape(1, p.hidden)
    b_out = jnp.pad(bias_out, (0, LANES - p.chans)).reshape(1, LANES)
    near, far = send_lat(p, even, blocks)

    columns = scratch((p.posp + 32, LANES), F32)
    deep = p.rows + 2 * REACH
    around = p.total + 2 * p.side
    taps_shape = sds((deep, around, p.wp, p.packed), BF16)
    act_shape = sds((p.rows + 2, p.total, p.wp, p.hidden), BF16)
    slope_shape = sds((p.rows + 2, p.total, p.wp, p.hidden), F32)
    inner = call(
        kernel(inner_kernel, p), [taps_shape, act_shape, slope_shape], [columns],
        [where, *blocks, w_in, b_in], 24 << 20, 6,
    )
    for bit in stages[1:]:
        goals = relay_tm(p, goals, bit)
    _, act, slope = call(
        kernel(outer_kernel, p), [taps_shape, act_shape, slope_shape], [columns],
        [where, near, far, w_in, b_in, *inner], 24 << 20, 8, {5: 0, 6: 1, 7: 2},
    )
    part = scratch((p.total, p.wp + 16, p.packed), F32)
    out = call(
        kernel(score_kernel, p),
        [sds((n, p.posp, LANES), F32)] + [sds((p.cp, p.posp), BF16)] * n,
        [part],
        [where, act, w_out, b_out, *goals], 24 << 20, 4,
    )
    wide, resids = out[0], out[1:]
    near, far = send_lat(p, even, resids)
    taps_shape = sds((deep, p.total, p.wp, p.packed), BF16)
    grad_shape = sds((p.rows + 2, around, p.wp, p.hidden), BF16)
    thin_rows = scratch((p.out, LANES), F32)
    out = call(
        kernel(back_inner_kernel, p),
        [taps_shape, grad_shape, sds((p.cp, p.out), F32)] + [sds((p.cp, p.out), BF16)] * (n - 1),
        [columns, thin_rows],
        [where, *resids, slope, w_out, wide], 24 << 20, 4,
    )
    taps, grad, scores = out[0], out[1], out[2:]
    taps, grad = call(
        kernel(back_outer_kernel, p), [taps_shape, grad_shape], [columns],
        [where, near, far, slope, w_out, taps, grad], 24 << 20, 3, {5: 0, 6: 1},
    )
    parts = [None] * n
    for d in [*range(n - 1, 0, -1), 0]:
        part = scratch((p.rows * p.local, p.wp + 16, p.packed), F32)
        parts[d] = call(
            kernel(guide_kernel, p, d), [sds((p.cp, 2 * p.out), scores[d].dtype)], [part, thin_rows],
            [where, grad, w_in, scores[d]], 16 << 20, 2,
        )[0]
        if d:
            parts[d] = send_tm(p, parts[d], d)
    shape = [sds((p.local, p.chans, p.rows, p.lon), F32)] * 2
    held = [scratch((n, p.cp, 2 * p.out), F32)]
    return tuple(call(kernel(join_kernel, p), shape, held, [where, *parts], 16 << 20, 1.5))


def solution(mesh):
    in_specs = (P("tm", None, "lat", None), P("tm", None, "lat", None), P(), P(), P(), P())
    out_specs = (P("tm", None, "lat", None), P("tm", None, "lat", None))
    return jax.shard_map(shards, mesh=mesh, in_specs=in_specs, out_specs=out_specs, check_vma=False)
```

```python
import functools

import jax
import jax.numpy as jnp
from jax import lax
from jax.experimental import pallas as pl
from jax.experimental.pallas import tpu as pltpu
from jax.sharding import PartitionSpec as P


F32 = jnp.float32
BF16 = jnp.bfloat16
LANES = 128
DEPTH = 4
REACH = 2
CODE = 14.0
VMEM = pl.BlockSpec(memory_space=pltpu.VMEM)
SMEM = pl.BlockSpec(memory_space=pltpu.SMEM)


def up(value, step):
    return -(-value // step) * step


class Plan:
    def __init__(self, states, conv_in):
        self.n = lax.axis_size("tm")
        self.m = lax.axis_size("lat")
        self.local, self.chans, self.rows, self.lon = states.shape
        self.taps = conv_in.shape[0]
        self.hidden = conv_in.shape[2]
        self.window = conv_in.shape[3] // self.chans
        self.side = self.window // 2
        self.total = self.local * self.n
        self.wc = self.lon // self.n
        self.wx = self.wc + 2 * DEPTH
        self.wp = up(self.wx, 16)
        self.cp = up(self.chans, 8)
        self.packed = 2 * LANES
        self.pos = self.rows * self.local * self.wx
        self.posp = up(self.pos, LANES)
        self.half = REACH * self.local * self.wx
        self.cut = (self.pos - self.half) // LANES * LANES
        self.msg = max(self.posp - self.cut, up(self.half, LANES))
        self.cut = self.posp - self.msg
        self.shift = self.pos - self.half - self.cut
        self.halfp = up(self.half, LANES)
        self.out = self.rows * self.local * self.wc
        assert self.taps == 3 and LANES <= 2 * self.chans and 3 * self.chans <= self.packed
        assert self.out % LANES == 0 and LANES % self.wc == 0 and self.wx % 8 == 0
        assert self.lon % LANES == 0 and self.rows == 2 * REACH and self.n & (self.n - 1) == 0

    def at(self, row, t):
        return (row * self.local + t) * self.wx

    def paired(self, row, t):
        return row // REACH * self.halfp + self.at(row % REACH, t)


def call(kernel, outs, scratch, args, limit, microseconds, aliases={}):
    return pl.pallas_call(
        kernel,
        out_shape=outs,
        in_specs=[SMEM if a.dtype == jnp.int32 else VMEM for a in args],
        out_specs=[VMEM] * len(outs),
        scratch_shapes=scratch,
        input_output_aliases=aliases,
        compiler_params=pltpu.CompilerParams(vmem_limit_bytes=limit),
        cost_estimate=pl.CostEstimate(flops=int(microseconds * 1e9), bytes_accessed=0, transcendentals=0),
    )(*args)


def lanes_of(shape):
    return lax.broadcasted_iota(jnp.int32, shape, len(shape) - 1)


def split_kernel(p, place, coded, where_ref, x_ref, *refs):
    outs, held = refs[: p.n], refs[p.n]
    me = where_ref[0]
    held[...] = jnp.zeros_like(held)
    for r in range(p.rows):
        for t in range(p.local):
            v = x_ref[t, :, r, :]
            start = place(r, t)
            base, off = start // LANES * LANES, start % LANES
            width = LANES if off + p.wx <= LANES else 2 * LANES
            lane = lanes_of((p.chans, width))
            inside = (lane >= off) & (lane < off + p.wx)
            for q in range(p.n):
                y = pltpu.roll(v, (off + DEPTH - p.wc * q) % p.lon, 1)[:, :width]
                old = held[q, : p.chans, base : base + width]
                held[q, : p.chans, base : base + width] = jnp.where(inside, y, old)
    for d in range(p.n):
        block = held[me ^ d]
        outs[d][...] = (jnp.exp(CODE * block) if coded else block).astype(BF16)


def weights_kernel(p, k_in, k_out, w_in, w_out, flat_ref, held):
    held[...] = jnp.zeros_like(held)
    c = p.chans
    for i in range(p.taps):
        for j in range(p.taps):
            flat_ref[j, : p.window * c] = k_in[i, j].astype(F32)
        for k in range(p.window):
            for j in range(p.taps):
                held[k, j * c : (j + 1) * c, :] = flat_ref[j, k * c : (k + 1) * c, :]
            w_in[i * p.window + k] = held[k].astype(BF16)
        for j in range(p.taps):
            held[p.window, j * c : (j + 1) * c, :] = k_out[i, j].astype(F32)
        w_out[i] = held[p.window].astype(BF16)


def to_columns(block, rows_ref):
    depth, width = block.shape
    for m in range(width // LANES):
        tile = block[:, m * LANES : (m + 1) * LANES].astype(F32)
        tile = jnp.concatenate([tile, jnp.zeros((LANES - depth, LANES), F32)], axis=0)
        rows_ref[8 + m * LANES : 8 + (m + 1) * LANES, :] = tile.T


def taps_of(p, rows_ref, start, flip):
    v = [rows_ref[8 + start + j : 8 + start + j + p.wp, :] for j in (-1, 0, 1)]
    if flip:
        v = v[::-1]
    lane = lanes_of((p.wp, LANES))
    middle = pltpu.roll(v[1], p.chans, 1)
    low = jnp.where(lane < p.chans, v[0], middle)
    high = jnp.where(lane < 2 * p.chans - LANES, middle, pltpu.roll(v[2], 2 * p.chans - LANES, 1))
    return jnp.concatenate([low, high], axis=1).astype(BF16)


def untap(p, ref, lead, start, count, flip):
    before, after = (1, -1) if flip else (-1, 1)
    s = start
    first = ref[lead, s + before : s + before + count, :LANES]
    low = pltpu.roll(ref[lead, s : s + count, :LANES], LANES - p.chans, 1)
    high = pltpu.roll(ref[lead, s : s + count, LANES:], LANES - p.chans, 1)
    lane = lanes_of((count, LANES))
    middle = jnp.where(lane < LANES - p.chans, low, high)
    last = pltpu.roll(ref[lead, s + after : s + after + count, LANES:], 2 * LANES - 2 * p.chans, 1)
    return jnp.where(lane < p.chans, first + middle + last, 0.0)


def fill_own(p, where_ref, blocks, rows_ref, taps_ref, flip, base):
    me = where_ref[0]
    for d in range(p.n):
        t0 = (me ^ d) * p.local + base
        to_columns(blocks[d][...], rows_ref)
        for r in range(p.rows):
            for t in range(p.local):
                taps_ref[REACH + r, t0 + t] = taps_of(p, rows_ref, p.at(r, t), flip)


def fill_halo(p, where_ref, near, far, rows_ref, taps_ref, flip, base):
    me, even = where_ref[0], where_ref[1] == 1
    for d in range(p.n):
        t0 = (me ^ d) * p.local + base
        to_columns(jnp.where(even, far[d], near[d]), rows_ref)
        for r in range(REACH):
            for t in range(p.local):
                taps_ref[r, t0 + t] = taps_of(p, rows_ref, p.shift + p.at(r, t), flip)
        to_columns(jnp.where(even, near[d], far[d]), rows_ref)
        for r in range(REACH):
            for t in range(p.local):
                taps_ref[REACH + p.rows + r, t0 + t] = taps_of(p, rows_ref, p.at(r, t), flip)


def fill_pairs(p, where_ref, halves, rows_ref, taps_ref, flip, row):
    me, even = where_ref[0], where_ref[1] == 1
    for d in range(p.n):
        to_columns(jnp.where(even, halves[0][d], halves[1][d]), rows_ref)
        for r in range(REACH):
            for t in range(p.local):
                taps_ref[row + r, (me ^ d) * p.local + t] = taps_of(p, rows_ref, p.at(r, t), flip)


def wrap(p, ref, begin, count):
    for row in range(begin, begin + count):
        for e in range(p.side):
            ref[row, e] = ref[row, p.total + e]
            ref[row, p.total + p.side + e] = ref[row, p.side + e]


def row_mask(p, where_ref, row):
    outside = ((row == 0) & (where_ref[2] == 1)) | ((row == p.rows + 1) & (where_ref[3] == 1))
    return jnp.where(outside, 0.0, 1.0)


def dot(a, b, transposed):
    dims = (((1,), (1 if transposed else 0,)), ((), ()))
    return lax.dot_general(a, b, dims, preferred_element_type=F32)


def hidden_rows(p, where_ref, taps_ref, w_in, bias_in, act_ref, slope_ref, count, row_of):
    def body(step, carry):
        row = row_of(step)
        total = None
        for i in range(p.taps):
            for k in range(p.window):
                a = taps_ref[row + i, k : k + p.total].reshape(p.total * p.wp, p.packed)
                term = dot(a, w_in[i * p.window + k], False)
                total = term if total is None else total + term
        pre = total + bias_in[...]
        sig = 0.5 * jnp.tanh(0.5 * pre) + 0.5
        act = pre * sig
        slope = sig + act * (1.0 - sig)
        mask = row_mask(p, where_ref, row)
        act_ref[row] = (act * mask).astype(BF16).reshape(p.total, p.wp, p.hidden)
        slope_ref[row] = (slope * mask).reshape(p.total, p.wp, p.hidden)
        return carry

    lax.fori_loop(0, count, body, 0)


def inner_kernel(p, where_ref, *refs):
    blocks, w_in, bias_in = refs[: p.n], refs[p.n], refs[p.n + 1]
    taps_ref, act_ref, slope_ref, rows_ref = refs[p.n + 2 :]
    fill_own(p, where_ref, blocks, rows_ref, taps_ref, False, p.side)
    wrap(p, taps_ref, REACH, p.rows)
    hidden_rows(p, where_ref, taps_ref, w_in, bias_in, act_ref, slope_ref, p.rows - 2, lambda s: s + REACH)


def outer_kernel(p, where_ref, near, far, w_in, bias_in, _taps, _act, _slope, taps_ref, act_ref, slope_ref, rows_ref):
    fill_halo(p, where_ref, near, far, rows_ref, taps_ref, False, p.side)
    wrap(p, taps_ref, 0, REACH)
    wrap(p, taps_ref, REACH + p.rows, REACH)
    edge = lambda s: jnp.where(s < REACH, s, s + p.rows - 2)
    hidden_rows(p, where_ref, taps_ref, w_in, bias_in, act_ref, slope_ref, 2 * REACH, edge)


def score_kernel(p, which, where_ref, *refs):
    n = p.n
    act_ref, w_out, bias_out = refs[:3]
    targets, wide_ref, resid_ref, part_ref = refs[3 : n + 3], refs[n + 3], refs[n + 4], refs[n + 5]
    me = where_ref[0]
    pair = 1 - where_ref[1] if which == 0 else where_ref[1]
    wide_ref[...] = jnp.zeros_like(wide_ref)

    def score_row(step, carry):
        total = None
        for i in range(p.taps):
            a = act_ref[pair * REACH + step + i].reshape(p.total * p.wp, p.hidden)
            term = dot(a, w_out[i], True)
            total = term if total is None else total + term
        part_ref[:, 8 : 8 + p.wp, :] = total.reshape(p.total, p.wp, p.packed)
        for d in range(n):
            for t in range(p.local):
                s = untap(p, part_ref, (me ^ d) * p.local + t, 8, p.wx, False) + bias_out[...]
                wide_ref[d, pl.ds(pl.multiple_of((step * p.local + t) * p.wx, 8), p.wx), :] = s
        return carry

    lax.fori_loop(0, REACH, score_row, 0)
    for d in range(n):
        for m in range(p.halfp // LANES):
            cols = slice(m * LANES, (m + 1) * LANES)
            tile = wide_ref[d, cols, :].T[: p.cp]
            target = targets[d][:, pl.ds(pl.multiple_of(pair * p.halfp + m * LANES, LANES), LANES)]
            resid_ref[d, :, cols] = (tile - jnp.log(target.astype(F32)) * (1.0 / CODE)).astype(BF16)


def gradient_rows(p, taps_ref, w_out, slope_ref, grad_ref, count, row_of):
    def body(step, carry):
        row = row_of(step)
        total = None
        for i in range(p.taps):
            a = taps_ref[row + 2 - i].reshape(p.total * p.wp, p.packed)
            term = dot(a, w_out[i], False)
            total = term if total is None else total + term
        grad = total.reshape(p.total, p.wp, p.hidden) * slope_ref[row]
        grad_ref[row, p.side : p.side + p.total] = grad.astype(BF16)
        return carry

    lax.fori_loop(0, count, body, 0)


def back_inner_kernel(p, where_ref, *refs):
    n = p.n
    resid, wide, slope_ref, w_out = refs[:2], refs[2:4], refs[4], refs[5]
    taps_ref, grad_ref = refs[6:8]
    own_ref, scores = refs[8], refs[9 : n + 8]
    rows_ref, thin_ref = refs[n + 8 :]
    even = where_ref[1] == 1
    fill_pairs(p, where_ref, resid, rows_ref, taps_ref, True, REACH)
    fill_pairs(p, where_ref, resid[::-1], rows_ref, taps_ref, True, 2 * REACH)
    gradient_rows(p, taps_ref, w_out, slope_ref, grad_ref, p.rows - 2, lambda s: s + REACH)
    wrap(p, grad_ref, REACH, p.rows - 2)
    for d in range(n):
        for r in range(p.rows):
            first, second = wide if r < REACH else wide[::-1]
            for t in range(p.local):
                start = p.at(r % REACH, t) + DEPTH
                at = (r * p.local + t) * p.wc
                here = slice(start, start + p.wc)
                thin_ref[at : at + p.wc, :] = jnp.where(even, first[d, here, :], second[d, here, :])
        turn(p, thin_ref, own_ref if d == 0 else scores[d - 1], 0)


def turn(p, thin_ref, out_ref, begin):
    for m in range(p.out // LANES):
        tile = thin_ref[m * LANES : (m + 1) * LANES, :].T[: p.cp]
        out_ref[:, begin + m * LANES : begin + (m + 1) * LANES] = tile.astype(out_ref.dtype)


def back_outer_kernel(p, where_ref, near, far, slope_ref, w_out, _taps, _grad, taps_ref, grad_ref, rows_ref):
    fill_pairs(p, where_ref, (far, near), rows_ref, taps_ref, True, 0)
    fill_pairs(p, where_ref, (near, far), rows_ref, taps_ref, True, 3 * REACH)
    edge = lambda s: jnp.where(s < REACH, s, s + p.rows - 2)
    gradient_rows(p, taps_ref, w_out, slope_ref, grad_ref, 2 * REACH, edge)
    wrap(p, grad_ref, 0, REACH)
    wrap(p, grad_ref, p.rows, REACH)


def guide_kernel(p, d, where_ref, grad_ref, w_in, *refs):
    out_ref, part_ref, thin_ref = refs[-3:]
    t0 = (where_ref[0] ^ d) * p.local
    total = None
    for i in range(p.taps):
        for k in range(p.window):
            a = grad_ref[2 - i : 2 - i + p.rows, pl.ds(t0 + 2 * p.side - k, p.local)]
            a = a.reshape(p.rows * p.local * p.wp, p.hidden)
            term = dot(a, w_in[i * p.window + k], True)
            total = term if total is None else total + term
    part_ref[:, 8 : 8 + p.wp, :] = total.reshape(p.rows * p.local, p.wp, p.packed)
    for r in range(p.rows * p.local):
        thin_ref[r * p.wc : (r + 1) * p.wc, :] = untap(p, part_ref, r, 8 + DEPTH, p.wc, True)
    turn(p, thin_ref, out_ref, 0)
    if len(refs) > 3:
        out_ref[:, p.out :] = refs[0][...]


def join_kernel(p, begins, where_ref, *refs):
    ins, out_ref, held = refs[: p.n], refs[p.n], refs[p.n + 1]
    me = where_ref[0]
    for d in range(p.n):
        held[me ^ d] = ins[d][:, begins[d] : begins[d] + p.out].astype(F32)
    per = LANES // p.wc
    lane = lanes_of((p.chans, LANES))
    for r in range(p.rows):
        for t in range(p.local):
            start = (r * p.local + t) * p.wc
            base, off = start // LANES * LANES, start % LANES
            for m in range(p.lon // LANES):
                tile = None
                for u in range(per):
                    piece = held[m * per + u, : p.chans, base : base + LANES]
                    step = (u * p.wc - off) % LANES
                    if step:
                        piece = pltpu.roll(piece, step, 1)
                    tile = piece if tile is None else jnp.where(lane < u * p.wc, tile, piece)
                out_ref[t, :, r, m * LANES : (m + 1) * LANES] = tile


def send_tm(p, value, d):
    return lax.ppermute(value, "tm", [(i, i ^ d) for i in range(p.n)])


def relay_tm(p, blocks, bit):
    moving = [d for d in range(p.n) if d & bit]
    moved = send_tm(p, jnp.stack([blocks[d] for d in moving]), bit)
    blocks = list(blocks)
    for at, d in enumerate(moving):
        blocks[d] = moved[at]
    return blocks


def send_near(p, value):
    return lax.ppermute(value, "lat", [(i, i ^ 1) for i in range(p.m)])


def send_far(p, value):
    return lax.ppermute(value, "lat", [(i, ((i + 1) ^ 1) - 1) for i in range(1, p.m - 1)])


def shards(states, observed, conv_in, bias_in, conv_out, bias_out):
    p = Plan(states, conv_in)
    n = p.n
    me, row = lax.axis_index("tm"), lax.axis_index("lat")
    even = row % 2 == 0
    where = jnp.stack([me, even.astype(jnp.int32), (row == 0).astype(jnp.int32), (row == p.m - 1).astype(jnp.int32)])
    where = where.astype(jnp.int32)
    sds = jax.ShapeDtypeStruct
    kernel = functools.partial
    scratch = pltpu.VMEM

    def split(field, place, coded, width):
        shape = [sds((p.cp, width), BF16)] * n
        held = [scratch((n, p.cp, width), F32)]
        return call(kernel(split_kernel, p, place, coded), shape, held, [where, field], 8 << 20, 1.5)

    mine = split(states, p.at, False, p.posp)
    blocks = [mine[0]] + [send_tm(p, mine[d], d) for d in range(1, n)]
    w_in, w_out = call(
        kernel(weights_kernel, p),
        [sds((p.taps * p.window, p.packed, p.hidden), BF16), sds((p.taps, p.packed, p.hidden), BF16)],
        [scratch((p.taps, up(p.window * p.chans, 8), p.hidden), F32), scratch((p.window + 1, p.packed, p.hidden), F32)],
        [jnp.swapaxes(conv_in, 2, 3), conv_out],
        16 << 20, 2,
    )
    goal = split(observed, p.paired, True, 2 * p.halfp)
    stages = [1 << b for b in range(n.bit_length() - 1)]
    goals = relay_tm(p, goal, stages[0])
    b_in = bias_in.reshape(1, p.hidden)
    b_out = jnp.pad(bias_out, (0, LANES - p.chans)).reshape(1, LANES)
    low = jnp.stack([b[:, : p.msg] for b in blocks])
    high = jnp.stack([b[:, p.cut :] for b in blocks])
    near = send_near(p, jnp.where(even, high, low))
    far = send_far(p, jnp.where(even, low, high))

    columns = scratch((p.posp + 32, LANES), F32)
    deep = p.rows + 2 * REACH
    around = p.total + 2 * p.side
    taps_shape = sds((deep, around, p.wp, p.packed), BF16)
    act_shape = sds((p.rows + 2, p.total, p.wp, p.hidden), BF16)
    slope_shape = sds((p.rows + 2, p.total, p.wp, p.hidden), F32)
    inner = call(
        kernel(inner_kernel, p), [taps_shape, act_shape, slope_shape], [columns],
        [where, *blocks, w_in, b_in], 24 << 20, 6,
    )
    for bit in stages[1:]:
        goals = relay_tm(p, goals, bit)
    _, act, slope = call(
        kernel(outer_kernel, p), [taps_shape, act_shape, slope_shape], [columns],
        [where, near, far, w_in, b_in, *inner], 24 << 20, 8, {5: 0, 6: 1, 7: 2},
    )
    part = scratch((p.total, p.wp + 16, p.packed), F32)

    def score(which):
        return call(
            kernel(score_kernel, p, which),
            [sds((n, p.halfp, LANES), F32), sds((n, p.cp, p.halfp), BF16)], [part],
            [where, act, w_out, b_out, *goals], 24 << 20, 2,
        )

    wide_far, resid_far = score(0)
    far = send_far(p, resid_far)
    wide_near, resid_near = score(1)
    near = send_near(p, resid_near)
    taps_shape = sds((deep, p.total, p.wp, p.packed), BF16)
    grad_shape = sds((p.rows + 2, around, p.wp, p.hidden), BF16)
    thin = sds((p.cp, p.out), BF16)
    thin_rows = scratch((p.out, LANES), F32)
    out = call(
        kernel(back_inner_kernel, p),
        [taps_shape, grad_shape, sds((p.cp, p.out), F32)] + [thin] * (n - 1),
        [columns, thin_rows],
        [where, resid_far, resid_near, wide_far, wide_near, slope, w_out], 32 << 20, 2.3,
    )
    taps, grad, scores = out[0], out[1], list(out[2:])
    scores[1] = send_tm(p, scores[1], 1)
    taps, grad = call(
        kernel(back_outer_kernel, p), [taps_shape, grad_shape], [columns],
        [where, near, far, slope, w_out, taps, grad], 24 << 20, 3, {5: 0, 6: 1},
    )
    parts = [None] * n
    for d in [*range(n - 1, 0, -1), 0]:
        spread = scratch((p.rows * p.local, p.wp + 16, p.packed), F32)
        ride = [scores[d]] if d > 1 else []
        shape = sds((p.cp, (1 + len(ride)) * p.out), BF16 if d else F32)
        parts[d] = call(
            kernel(guide_kernel, p, d), [shape], [spread, thin_rows],
            [where, grad, w_in, *ride], 16 << 20, 2,
        )[0]
        if d:
            parts[d] = send_tm(p, parts[d], d)

    def join(blocks, begins):
        shape = [sds((p.local, p.chans, p.rows, p.lon), F32)]
        held = [scratch((n, p.cp, p.out), F32)]
        return call(kernel(join_kernel, p, begins), shape, held, [where, *blocks], 8 << 20, 1)[0]

    begins = [0, 0] + [p.out] * (n - 2)
    return join(scores[:2] + parts[2:], begins), join(parts, [0] * n)


def solution(mesh):
    in_specs = (P("tm", None, "lat", None), P("tm", None, "lat", None), P(), P(), P(), P())
    out_specs = (P("tm", None, "lat", None), P("tm", None, "lat", None))
    return jax.shard_map(shards, mesh=mesh, in_specs=in_specs, out_specs=out_specs, check_vma=False)
```

```python
import functools

import jax
import jax.numpy as jnp
from jax import lax
from jax.experimental import pallas as pl
from jax.experimental.pallas import tpu as pltpu
from jax.sharding import PartitionSpec as P


F32 = jnp.float32
BF16 = jnp.bfloat16
LANES = 128
DEPTH = 4
REACH = 2
CODE = 14.0
VMEM = pl.BlockSpec(memory_space=pltpu.VMEM)


def up(value, step):
    return -(-value // step) * step


class Plan:
    def __init__(self, states, conv_in):
        self.n = lax.axis_size("tm")
        self.m = lax.axis_size("lat")
        self.local, self.chans, self.rows, self.lon = states.shape
        self.taps = conv_in.shape[0]
        self.hidden = conv_in.shape[2]
        self.window = conv_in.shape[3] // self.chans
        self.side = self.window // 2
        self.total = self.local * self.n
        self.wc = self.lon // self.n
        self.wx = self.wc + 2 * DEPTH
        self.wp = up(self.wx, 16)
        self.cp = up(self.chans, 8)
        self.packed = 2 * LANES
        self.pos = self.rows * self.local * self.wx
        self.posp = up(self.pos, LANES)
        self.half = REACH * self.local * self.wx
        self.cut = (self.pos - self.half) // LANES * LANES
        self.msg = max(self.posp - self.cut, up(self.half, LANES))
        self.cut = self.posp - self.msg
        self.shift = self.pos - self.half - self.cut
        self.halfp = up(self.half, LANES)
        self.out = self.rows * self.local * self.wc
        assert self.taps == 3 and LANES <= 2 * self.chans and 3 * self.chans <= self.packed
        assert self.out % LANES == 0 and LANES % self.wc == 0 and self.wx % 8 == 0
        assert self.lon % LANES == 0 and self.rows == 2 * REACH and self.n & (self.n - 1) == 0

    def at(self, row, t):
        return (row * self.local + t) * self.wx

    def paired(self, row, t):
        return row // REACH * self.halfp + self.at(row % REACH, t)


def here():
    row = lax.axis_index("lat")
    flags = [row % 2 == 0, row == 0, row == lax.axis_size("lat") - 1]
    return [lax.axis_index("tm")] + [flag.astype(jnp.int32) for flag in flags]


def call(kernel, outs, scratch, args, limit, microseconds, aliases={}):
    return pl.pallas_call(
        lambda *refs: kernel(here(), *refs),
        out_shape=outs,
        in_specs=[VMEM] * len(args),
        out_specs=[VMEM] * len(outs),
        scratch_shapes=scratch,
        input_output_aliases=aliases,
        compiler_params=pltpu.CompilerParams(vmem_limit_bytes=limit),
        cost_estimate=pl.CostEstimate(flops=int(microseconds * 1e9), bytes_accessed=0, transcendentals=0),
    )(*args)


def lanes_of(shape):
    return lax.broadcasted_iota(jnp.int32, shape, len(shape) - 1)


def split_kernel(p, place, coded, where, x_ref, *refs):
    outs, held = refs[: p.n], refs[p.n]
    me = where[0]
    held[...] = jnp.zeros_like(held)
    for r in range(p.rows):
        for t in range(p.local):
            v = x_ref[t, :, r, :]
            start = place(r, t)
            base, off = start // LANES * LANES, start % LANES
            width = LANES if off + p.wx <= LANES else 2 * LANES
            lane = lanes_of((p.chans, width))
            inside = (lane >= off) & (lane < off + p.wx)
            for q in range(p.n):
                y = pltpu.roll(v, (off + DEPTH - p.wc * q) % p.lon, 1)[:, :width]
                old = held[q, : p.chans, base : base + width]
                held[q, : p.chans, base : base + width] = jnp.where(inside, y, old)
    for d in range(p.n):
        block = held[me ^ d]
        outs[d][...] = (jnp.exp(CODE * block) if coded else block).astype(BF16)


def weights_kernel(p, where, k_in, k_out, w_in, w_out, flat_ref, held):
    held[...] = jnp.zeros_like(held)
    c = p.chans
    for i in range(p.taps):
        for j in range(p.taps):
            flat_ref[j, : p.window * c] = k_in[i, j].astype(F32)
        for k in range(p.window):
            for j in range(p.taps):
                held[k, j * c : (j + 1) * c, :] = flat_ref[j, k * c : (k + 1) * c, :]
            w_in[i * p.window + k] = held[k].astype(BF16)
        for j in range(p.taps):
            held[p.window, j * c : (j + 1) * c, :] = k_out[i, j].astype(F32)
        w_out[i] = held[p.window].astype(BF16)


def to_columns(block, rows_ref):
    depth, width = block.shape
    for m in range(width // LANES):
        tile = block[:, m * LANES : (m + 1) * LANES].astype(F32)
        tile = jnp.concatenate([tile, jnp.zeros((LANES - depth, LANES), F32)], axis=0)
        rows_ref[8 + m * LANES : 8 + (m + 1) * LANES, :] = tile.T


def taps_of(p, rows_ref, start, flip):
    v = [rows_ref[8 + start + j : 8 + start + j + p.wp, :] for j in (-1, 0, 1)]
    if flip:
        v = v[::-1]
    lane = lanes_of((p.wp, LANES))
    middle = pltpu.roll(v[1], p.chans, 1)
    low = jnp.where(lane < p.chans, v[0], middle)
    high = jnp.where(lane < 2 * p.chans - LANES, middle, pltpu.roll(v[2], 2 * p.chans - LANES, 1))
    return jnp.concatenate([low, high], axis=1).astype(BF16)


def spread(p, total, parts):
    lead = total.shape[0] // p.wp
    for tile, ref in enumerate(parts):
        ref[:, 8 : 8 + p.wp, :] = total[:, tile * LANES : (tile + 1) * LANES].reshape(lead, p.wp, LANES)


def untap(p, parts, lead, start, count, flip):
    before, after = (1, -1) if flip else (-1, 1)
    first = parts[0][lead, start + before : start + before + count, :]
    low = pltpu.roll(parts[0][lead, start : start + count, :], LANES - p.chans, 1)
    high = pltpu.roll(parts[1][lead, start : start + count, :], LANES - p.chans, 1)
    lane = lanes_of((count, LANES))
    middle = jnp.where(lane < LANES - p.chans, low, high)
    last = pltpu.roll(parts[1][lead, start + after : start + after + count, :], 2 * LANES - 2 * p.chans, 1)
    return jnp.where(lane < p.chans, first + middle + last, 0.0)


def fill_own(p, where, blocks, rows_ref, taps_ref, flip, base):
    me = where[0]
    for d in range(p.n):
        t0 = (me ^ d) * p.local + base
        to_columns(blocks[d][...], rows_ref)
        for r in range(p.rows):
            for t in range(p.local):
                taps_ref[REACH + r, t0 + t] = taps_of(p, rows_ref, p.at(r, t), flip)


def fill_halo(p, where, near, far, rows_ref, taps_ref, flip, base):
    me, even = where[0], where[1] == 1
    for d in range(p.n):
        t0 = (me ^ d) * p.local + base
        to_columns(jnp.where(even, far[d], near[d]), rows_ref)
        for r in range(REACH):
            for t in range(p.local):
                taps_ref[r, t0 + t] = taps_of(p, rows_ref, p.shift + p.at(r, t), flip)
        to_columns(jnp.where(even, near[d], far[d]), rows_ref)
        for r in range(REACH):
            for t in range(p.local):
                taps_ref[REACH + p.rows + r, t0 + t] = taps_of(p, rows_ref, p.at(r, t), flip)


def fill_pairs(p, where, halves, rows_ref, taps_ref, flip, row):
    me, even = where[0], where[1] == 1
    for d in range(p.n):
        to_columns(jnp.where(even, halves[0][d], halves[1][d]), rows_ref)
        for r in range(REACH):
            for t in range(p.local):
                taps_ref[row + r, (me ^ d) * p.local + t] = taps_of(p, rows_ref, p.at(r, t), flip)


def wrap(p, ref, begin, count):
    for row in range(begin, begin + count):
        for e in range(p.side):
            ref[row, e] = ref[row, p.total + e]
            ref[row, p.total + p.side + e] = ref[row, p.side + e]


def row_mask(p, where, row):
    outside = ((row == 0) & (where[2] == 1)) | ((row == p.rows + 1) & (where[3] == 1))
    return jnp.where(outside, 0.0, 1.0)


def dot(a, b, transposed):
    dims = (((1,), (1 if transposed else 0,)), ((), ()))
    return lax.dot_general(a, b, dims, preferred_element_type=F32)


def hidden_rows(p, where, taps_ref, w_in, bias_in, act_ref, slope_ref, count, row_of):
    def body(step, carry):
        row = row_of(step)
        total = None
        for i in range(p.taps):
            for k in range(p.window):
                a = taps_ref[row + i, k : k + p.total].reshape(p.total * p.wp, p.packed)
                term = dot(a, w_in[i * p.window + k], False)
                total = term if total is None else total + term
        pre = total + bias_in[...]
        sig = 0.5 * jnp.tanh(0.5 * pre) + 0.5
        act = pre * sig
        slope = sig + act * (1.0 - sig)
        mask = row_mask(p, where, row)
        act_ref[row] = (act * mask).astype(BF16).reshape(p.total, p.wp, p.hidden)
        slope_ref[row] = (slope * mask).reshape(p.total, p.wp, p.hidden)
        return carry

    lax.fori_loop(0, count, body, 0)


def inner_kernel(p, where, *refs):
    blocks, w_in, bias_in = refs[: p.n], refs[p.n], refs[p.n + 1]
    taps_ref, act_ref, slope_ref, rows_ref = refs[p.n + 2 :]
    fill_own(p, where, blocks, rows_ref, taps_ref, False, p.side)
    wrap(p, taps_ref, REACH, p.rows)
    hidden_rows(p, where, taps_ref, w_in, bias_in, act_ref, slope_ref, p.rows - 2, lambda s: s + REACH)


def outer_kernel(p, where, near, far, w_in, bias_in, _taps, _act, _slope, taps_ref, act_ref, slope_ref, rows_ref):
    fill_halo(p, where, near, far, rows_ref, taps_ref, False, p.side)
    wrap(p, taps_ref, 0, REACH)
    wrap(p, taps_ref, REACH + p.rows, REACH)
    edge = lambda s: jnp.where(s < REACH, s, s + p.rows - 2)
    hidden_rows(p, where, taps_ref, w_in, bias_in, act_ref, slope_ref, 2 * REACH, edge)


def score_kernel(p, which, where, *refs):
    n = p.n
    act_ref, w_out, bias_out = refs[:3]
    targets, wide_ref, resid_ref, parts = refs[3 : n + 3], refs[n + 3], refs[n + 4], refs[n + 5 :]
    me = where[0]
    pair = 1 - where[1] if which == 0 else where[1]
    wide_ref[...] = jnp.zeros_like(wide_ref)

    def score_row(step, carry):
        total = None
        for i in range(p.taps):
            a = act_ref[pair * REACH + step + i].reshape(p.total * p.wp, p.hidden)
            term = dot(a, w_out[i], True)
            total = term if total is None else total + term
        spread(p, total, parts)
        for d in range(n):
            for t in range(p.local):
                s = untap(p, parts, (me ^ d) * p.local + t, 8, p.wx, False) + bias_out[...]
                wide_ref[d, pl.ds(pl.multiple_of((step * p.local + t) * p.wx, 8), p.wx), :] = s
        return carry

    lax.fori_loop(0, REACH, score_row, 0)
    for d in range(n):
        for m in range(p.halfp // LANES):
            cols = slice(m * LANES, (m + 1) * LANES)
            tile = wide_ref[d, cols, :].T[: p.cp]
            target = targets[d][:, pl.ds(pl.multiple_of(pair * p.halfp + m * LANES, LANES), LANES)]
            resid_ref[d, :, cols] = (tile - jnp.log(target.astype(F32)) * (1.0 / CODE)).astype(BF16)


def gradient_rows(p, taps_ref, w_out, slope_ref, grad_ref, count, row_of):
    def body(step, carry):
        row = row_of(step)
        total = None
        for i in range(p.taps):
            a = taps_ref[row + 2 - i].reshape(p.total * p.wp, p.packed)
            term = dot(a, w_out[i], False)
            total = term if total is None else total + term
        grad = total.reshape(p.total, p.wp, p.hidden) * slope_ref[row]
        grad_ref[row, p.side : p.side + p.total] = grad.astype(BF16)
        return carry

    lax.fori_loop(0, count, body, 0)


def back_inner_kernel(p, where, *refs):
    n = p.n
    resid, wide, slope_ref, w_out = refs[:2], refs[2:4], refs[4], refs[5]
    taps_ref, grad_ref = refs[6:8]
    own_ref, scores = refs[8], refs[9 : n + 8]
    rows_ref, thin_ref = refs[n + 8 :]
    even = where[1] == 1
    fill_pairs(p, where, resid, rows_ref, taps_ref, True, REACH)
    fill_pairs(p, where, resid[::-1], rows_ref, taps_ref, True, 2 * REACH)
    gradient_rows(p, taps_ref, w_out, slope_ref, grad_ref, p.rows - 2, lambda s: s + REACH)
    wrap(p, grad_ref, REACH, p.rows - 2)
    for d in range(n):
        for r in range(p.rows):
            first, second = wide if r < REACH else wide[::-1]
            for t in range(p.local):
                start = p.at(r % REACH, t) + DEPTH
                at = (r * p.local + t) * p.wc
                here = slice(start, start + p.wc)
                thin_ref[at : at + p.wc, :] = jnp.where(even, first[d, here, :], second[d, here, :])
        turn(p, thin_ref, own_ref if d == 0 else scores[d - 1], 0)


def turn(p, thin_ref, out_ref, begin):
    for m in range(p.out // LANES):
        tile = thin_ref[m * LANES : (m + 1) * LANES, :].T[: p.cp]
        out_ref[:, begin + m * LANES : begin + (m + 1) * LANES] = tile.astype(out_ref.dtype)


def back_outer_kernel(p, where, near, far, slope_ref, w_out, _taps, _grad, taps_ref, grad_ref, rows_ref):
    fill_pairs(p, where, (far, near), rows_ref, taps_ref, True, 0)
    fill_pairs(p, where, (near, far), rows_ref, taps_ref, True, 3 * REACH)
    edge = lambda s: jnp.where(s < REACH, s, s + p.rows - 2)
    gradient_rows(p, taps_ref, w_out, slope_ref, grad_ref, 2 * REACH, edge)
    wrap(p, grad_ref, 0, REACH)
    wrap(p, grad_ref, p.rows, REACH)


def guide_kernel(p, d, where, grad_ref, w_in, *refs):
    out_ref, thin_ref, parts = refs[-4], refs[-3], refs[-2:]
    t0 = (where[0] ^ d) * p.local
    total = None
    for i in range(p.taps):
        for k in range(p.window):
            a = grad_ref[2 - i : 2 - i + p.rows, pl.ds(t0 + 2 * p.side - k, p.local)]
            a = a.reshape(p.rows * p.local * p.wp, p.hidden)
            term = dot(a, w_in[i * p.window + k], True)
            total = term if total is None else total + term
    spread(p, total, parts)
    for r in range(p.rows * p.local):
        thin_ref[r * p.wc : (r + 1) * p.wc, :] = untap(p, parts, r, 8 + DEPTH, p.wc, True)
    turn(p, thin_ref, out_ref, 0)
    if len(refs) > 4:
        out_ref[:, p.out :] = refs[0][...]


def join_kernel(p, begins, where, *refs):
    ins, out_ref, held = refs[: p.n], refs[p.n], refs[p.n + 1]
    me = where[0]
    for d in range(p.n):
        held[me ^ d] = ins[d][:, begins[d] : begins[d] + p.out].astype(F32)
    per = LANES // p.wc
    lane = lanes_of((p.chans, LANES))
    for r in range(p.rows):
        for t in range(p.local):
            start = (r * p.local + t) * p.wc
            base, off = start // LANES * LANES, start % LANES
            for m in range(p.lon // LANES):
                tile = None
                for u in range(per):
                    piece = held[m * per + u, : p.chans, base : base + LANES]
                    step = (u * p.wc - off) % LANES
                    if step:
                        piece = pltpu.roll(piece, step, 1)
                    tile = piece if tile is None else jnp.where(lane < u * p.wc, tile, piece)
                out_ref[t, :, r, m * LANES : (m + 1) * LANES] = tile


def send_tm(p, value, d):
    return lax.ppermute(value, "tm", [(i, i ^ d) for i in range(p.n)])


def relay_tm(p, blocks, bit):
    moving = [d for d in range(p.n) if d & bit]
    moved = send_tm(p, jnp.stack([blocks[d] for d in moving]), bit)
    blocks = list(blocks)
    for at, d in enumerate(moving):
        blocks[d] = moved[at]
    return blocks


def send_near(p, value):
    return lax.ppermute(value, "lat", [(i, i ^ 1) for i in range(p.m)])


def send_far(p, value):
    return lax.ppermute(value, "lat", [(i, ((i + 1) ^ 1) - 1) for i in range(1, p.m - 1)])


def shards(states, observed, conv_in, bias_in, conv_out, bias_out):
    p = Plan(states, conv_in)
    n = p.n
    even = lax.axis_index("lat") % 2 == 0
    sds = jax.ShapeDtypeStruct
    kernel = functools.partial
    scratch = pltpu.VMEM

    def split(field, place, coded, width):
        shape = [sds((p.cp, width), BF16)] * n
        held = [scratch((n, p.cp, width), F32)]
        return call(kernel(split_kernel, p, place, coded), shape, held, [field], 8 << 20, 1.5)

    mine = split(states, p.at, False, p.posp)
    blocks = [mine[0]] + [send_tm(p, mine[d], d) for d in range(1, n)]
    w_in, w_out = call(
        kernel(weights_kernel, p),
        [sds((p.taps * p.window, p.packed, p.hidden), BF16), sds((p.taps, p.packed, p.hidden), BF16)],
        [scratch((p.taps, up(p.window * p.chans, 8), p.hidden), F32), scratch((p.window + 1, p.packed, p.hidden), F32)],
        [jnp.swapaxes(conv_in, 2, 3), conv_out],
        16 << 20, 2,
    )
    goal = split(observed, p.paired, True, 2 * p.halfp)
    stages = [1 << b for b in range(n.bit_length() - 1)]
    goals = relay_tm(p, goal, stages[0])
    b_in = bias_in.reshape(1, p.hidden)
    b_out = jnp.pad(bias_out, (0, LANES - p.chans)).reshape(1, LANES)
    low = jnp.stack([b[:, : p.msg] for b in blocks])
    high = jnp.stack([b[:, p.cut :] for b in blocks])
    near = send_near(p, jnp.where(even, high, low))
    far = send_far(p, jnp.where(even, low, high))

    columns = scratch((p.posp + 32, LANES), F32)
    deep = p.rows + 2 * REACH
    around = p.total + 2 * p.side
    taps_shape = sds((deep, around, p.wp, p.packed), BF16)
    act_shape = sds((p.rows + 2, p.total, p.wp, p.hidden), BF16)
    slope_shape = sds((p.rows + 2, p.total, p.wp, p.hidden), F32)
    inner = call(
        kernel(inner_kernel, p), [taps_shape, act_shape, slope_shape], [columns],
        [*blocks, w_in, b_in], 24 << 20, 6,
    )
    for bit in stages[1:]:
        goals = relay_tm(p, goals, bit)
    _, act, slope = call(
        kernel(outer_kernel, p), [taps_shape, act_shape, slope_shape], [columns],
        [near, far, w_in, b_in, *inner], 24 << 20, 8, {4: 0, 5: 1, 6: 2},
    )
    part = [scratch((p.total, p.wp + 16, LANES), F32)] * 2

    def score(which):
        return call(
            kernel(score_kernel, p, which),
            [sds((n, p.halfp, LANES), F32), sds((n, p.cp, p.halfp), BF16)], part,
            [act, w_out, b_out, *goals], 24 << 20, 2,
        )

    wide_far, resid_far = score(0)
    far = send_far(p, resid_far)
    wide_near, resid_near = score(1)
    near = send_near(p, resid_near)
    taps_shape = sds((deep, p.total, p.wp, p.packed), BF16)
    grad_shape = sds((p.rows + 2, around, p.wp, p.hidden), BF16)
    thin = sds((p.cp, p.out), BF16)
    thin_rows = scratch((p.out, LANES), F32)
    out = call(
        kernel(back_inner_kernel, p),
        [taps_shape, grad_shape, sds((p.cp, p.out), F32)] + [thin] * (n - 1),
        [columns, thin_rows],
        [resid_far, resid_near, wide_far, wide_near, slope, w_out], 32 << 20, 2.3,
    )
    taps, grad, scores = out[0], out[1], list(out[2:])
    scores[1] = send_tm(p, scores[1], 1)
    taps, grad = call(
        kernel(back_outer_kernel, p), [taps_shape, grad_shape], [columns],
        [near, far, slope, w_out, taps, grad], 24 << 20, 3, {4: 0, 5: 1},
    )
    parts = [None] * n
    for d in [*range(n - 1, 0, -1), 0]:
        part = [scratch((p.rows * p.local, p.wp + 16, LANES), F32)] * 2
        ride = [scores[d]] if d > 1 else []
        shape = sds((p.cp, (1 + len(ride)) * p.out), BF16 if d else F32)
        parts[d] = call(
            kernel(guide_kernel, p, d), [shape], [thin_rows, *part],
            [grad, w_in, *ride], 16 << 20, 2,
        )[0]
        if d:
            parts[d] = send_tm(p, parts[d], d)

    def join(blocks, begins):
        shape = [sds((p.local, p.chans, p.rows, p.lon), F32)]
        held = [scratch((n, p.cp, p.out), F32)]
        return call(kernel(join_kernel, p, begins), shape, held, [*blocks], 8 << 20, 1)[0]

    begins = [0, 0] + [p.out] * (n - 2)
    return join(scores[:2] + parts[2:], begins), join(parts, [0] * n)


def solution(mesh):
    in_specs = (P("tm", None, "lat", None), P("tm", None, "lat", None), P(), P(), P(), P())
    out_specs = (P("tm", None, "lat", None), P("tm", None, "lat", None))
    return jax.shard_map(shards, mesh=mesh, in_specs=in_specs, out_specs=out_specs, check_vma=False)
```

```python
import functools

import jax
import jax.numpy as jnp
from jax import lax
from jax.experimental import pallas as pl
from jax.experimental.pallas import tpu as pltpu
from jax.sharding import PartitionSpec as P


F32 = jnp.float32
BF16 = jnp.bfloat16
LANES = 128
DEPTH = 4
REACH = 2
CODE = 14.0
VMEM = pl.BlockSpec(memory_space=pltpu.VMEM)


def up(value, step):
    return -(-value // step) * step


class Plan:
    def __init__(self, states, conv_in):
        self.n = lax.axis_size("tm")
        self.m = lax.axis_size("lat")
        self.local, self.chans, self.rows, self.lon = states.shape
        self.taps = conv_in.shape[0]
        self.hidden = conv_in.shape[2]
        self.window = conv_in.shape[3] // self.chans
        self.side = self.window // 2
        self.total = self.local * self.n
        self.wc = self.lon // self.n
        self.wx = self.wc + 2 * DEPTH
        self.wp = up(self.wx, 16)
        self.cp = up(self.chans, 8)
        self.packed = 2 * LANES
        self.pos = self.rows * self.local * self.wx
        self.posp = up(self.pos, LANES)
        self.half = REACH * self.local * self.wx
        self.cut = (self.pos - self.half) // LANES * LANES
        self.msg = max(self.posp - self.cut, up(self.half, LANES))
        self.cut = self.posp - self.msg
        self.shift = self.pos - self.half - self.cut
        self.halfp = up(self.half, LANES)
        self.out = self.rows * self.local * self.wc
        assert self.taps == 3 and LANES <= 2 * self.chans and 3 * self.chans <= self.packed
        assert self.out % LANES == 0 and LANES % self.wc == 0 and self.wx % 8 == 0
        assert self.lon % LANES == 0 and self.rows == 2 * REACH and self.n & (self.n - 1) == 0

    def at(self, row, t):
        return (row * self.local + t) * self.wx

    def paired(self, row, t):
        return row // REACH * self.halfp + self.at(row % REACH, t)


def here():
    row = lax.axis_index("lat")
    flags = [row % 2 == 0, row == 0, row == lax.axis_size("lat") - 1]
    return [lax.axis_index("tm")] + [flag.astype(jnp.int32) for flag in flags]


def call(kernel, outs, scratch, args, limit, microseconds, aliases={}, states=0, ins_by=False, outs_by=False):
    def one(shape):
        return pl.BlockSpec((1,) + tuple(shape[1:]), lambda t: (t,) + (0,) * (len(shape) - 1))

    return pl.pallas_call(
        lambda *refs: kernel(here(), *refs),
        grid=(states,) if states else (),
        out_shape=outs,
        in_specs=[one(a.shape) if ins_by else VMEM for a in args],
        out_specs=[one(a.shape) if outs_by else VMEM for a in outs],
        scratch_shapes=scratch,
        input_output_aliases=aliases,
        compiler_params=pltpu.CompilerParams(vmem_limit_bytes=limit),
        cost_estimate=pl.CostEstimate(flops=int(microseconds * 1e9), bytes_accessed=0, transcendentals=0),
    )(*args)


def lanes_of(shape):
    return lax.broadcasted_iota(jnp.int32, shape, len(shape) - 1)


def split_kernel(p, place, coded, where, x_ref, *refs):
    outs, held = refs[: p.n], refs[p.n]

    @pl.when(pl.program_id(0) == 0)
    def _():
        held[...] = jnp.zeros_like(held)

    def place_state(t):
        for r in range(p.rows):
            v = x_ref[0, :, r, :]
            start = place(r, t)
            base, off = start // LANES * LANES, start % LANES
            width = LANES if off + p.wx <= LANES else 2 * LANES
            lane = lanes_of((p.chans, width))
            inside = (lane >= off) & (lane < off + p.wx)
            for q in range(p.n):
                y = pltpu.roll(v, (off + DEPTH - p.wc * q) % p.lon, 1)[:, :width]
                old = held[q, : p.chans, base : base + width]
                held[q, : p.chans, base : base + width] = jnp.where(inside, y, old)

    for t in range(p.local):
        pl.when(pl.program_id(0) == t)(functools.partial(place_state, t))

    @pl.when(pl.program_id(0) == p.local - 1)
    def _():
        for d in range(p.n):
            block = held[where[0] ^ d]
            outs[d][...] = (jnp.exp(CODE * block) if coded else block).astype(BF16)


def weights_kernel(p, where, k_in, k_out, w_in, w_out, flat_ref, held):
    held[...] = jnp.zeros_like(held)
    c = p.chans
    for i in range(p.taps):
        for j in range(p.taps):
            flat_ref[j, : p.window * c] = k_in[i, j].astype(F32)
        for k in range(p.window):
            for j in range(p.taps):
                held[k, j * c : (j + 1) * c, :] = flat_ref[j, k * c : (k + 1) * c, :]
            w_in[i * p.window + k] = held[k].astype(BF16)
        for j in range(p.taps):
            held[p.window, j * c : (j + 1) * c, :] = k_out[i, j].astype(F32)
        w_out[i] = held[p.window].astype(BF16)


def to_columns(block, rows_ref):
    depth, width = block.shape
    for m in range(width // LANES):
        tile = block[:, m * LANES : (m + 1) * LANES]
        tile = jnp.concatenate([tile, jnp.zeros((LANES - depth, LANES), BF16)], axis=0)
        rows_ref[8 + m * LANES : 8 + (m + 1) * LANES, :] = tile.T.astype(F32)


def taps_of(p, rows_ref, start, flip):
    v = [rows_ref[8 + start + j : 8 + start + j + p.wp, :].astype(BF16) for j in (-1, 0, 1)]
    if flip:
        v = v[::-1]
    lane = lanes_of((p.wp, LANES))
    middle = pltpu.roll(v[1], p.chans, 1)
    low = jnp.where(lane < p.chans, v[0], middle)
    high = jnp.where(lane < 2 * p.chans - LANES, middle, pltpu.roll(v[2], 2 * p.chans - LANES, 1))
    return jnp.concatenate([low, high], axis=1)


def spread(p, total, parts):
    lead = total.shape[0] // p.wp
    for tile, ref in enumerate(parts):
        ref[:, 8 : 8 + p.wp, :] = total[:, tile * LANES : (tile + 1) * LANES].reshape(lead, p.wp, LANES)


def untap(p, parts, lead, start, count, flip):
    before, after = (1, -1) if flip else (-1, 1)
    first = parts[0][lead, start + before : start + before + count, :]
    low = pltpu.roll(parts[0][lead, start : start + count, :], LANES - p.chans, 1)
    high = pltpu.roll(parts[1][lead, start : start + count, :], LANES - p.chans, 1)
    lane = lanes_of((count, LANES))
    middle = jnp.where(lane < LANES - p.chans, low, high)
    last = pltpu.roll(parts[1][lead, start + after : start + after + count, :], 2 * LANES - 2 * p.chans, 1)
    return jnp.where(lane < p.chans, first + middle + last, 0.0)


def fill_own(p, where, blocks, rows_ref, taps_ref, flip, base):
    me = where[0]
    for d, block in blocks.items():
        t0 = (me ^ d) * p.local + base
        to_columns(block[...], rows_ref)
        for r in range(p.rows):
            for t in range(p.local):
                taps_ref[REACH + r, t0 + t] = taps_of(p, rows_ref, p.at(r, t), flip)


def fill_halo(p, where, near, far, rows_ref, taps_ref, flip, base):
    me, even = where[0], where[1] == 1
    for d in range(p.n):
        t0 = (me ^ d) * p.local + base
        to_columns(jnp.where(even, far[d], near[d]), rows_ref)
        for r in range(REACH):
            for t in range(p.local):
                taps_ref[r, t0 + t] = taps_of(p, rows_ref, p.shift + p.at(r, t), flip)
        to_columns(jnp.where(even, near[d], far[d]), rows_ref)
        for r in range(REACH):
            for t in range(p.local):
                taps_ref[REACH + p.rows + r, t0 + t] = taps_of(p, rows_ref, p.at(r, t), flip)


def fill_pairs(p, where, halves, rows_ref, taps_ref, flip, row):
    me, even = where[0], where[1] == 1
    for d in range(p.n):
        to_columns(jnp.where(even, halves[0][d], halves[1][d]), rows_ref)
        for r in range(REACH):
            for t in range(p.local):
                taps_ref[row + r, (me ^ d) * p.local + t] = taps_of(p, rows_ref, p.at(r, t), flip)


def wrap(p, ref, begin, count):
    for row in range(begin, begin + count):
        for e in range(p.side):
            ref[row, e] = ref[row, p.total + e]
            ref[row, p.total + p.side + e] = ref[row, p.side + e]


def row_mask(p, where, row):
    outside = ((row == 0) & (where[2] == 1)) | ((row == p.rows + 1) & (where[3] == 1))
    return jnp.where(outside, 0.0, 1.0)


def dot(a, b, transposed):
    dims = (((1,), (1 if transposed else 0,)), ((), ()))
    return lax.dot_general(a, b, dims, preferred_element_type=F32)


def hidden_rows(p, where, taps_ref, w_in, bias_in, act_ref, slope_ref, count, row_of):
    def body(step, carry):
        row = row_of(step)
        total = None
        for i in range(p.taps):
            for k in range(p.window):
                a = taps_ref[row + i, k : k + p.total].reshape(p.total * p.wp, p.packed)
                term = dot(a, w_in[i * p.window + k], False)
                total = term if total is None else total + term
        pre = total + bias_in[...]
        sig = 0.5 * jnp.tanh(0.5 * pre) + 0.5
        act = pre * sig
        slope = sig + act * (1.0 - sig)
        mask = row_mask(p, where, row)
        act_ref[row] = (act * mask).astype(BF16).reshape(p.total, p.wp, p.hidden)
        slope_ref[row] = (slope * mask).reshape(p.total, p.wp, p.hidden)
        return carry

    lax.fori_loop(0, count, body, 0)


def early_kernel(p, where, *refs):
    blocks, taps_ref, rows_ref = refs[: p.n - 1], refs[p.n - 1], refs[p.n]
    fill_own(p, where, dict(enumerate(blocks)), rows_ref, taps_ref, False, p.side)


def inner_kernel(p, where, block, w_in, bias_in, _taps, taps_ref, act_ref, slope_ref, rows_ref):
    fill_own(p, where, {p.n - 1: block}, rows_ref, taps_ref, False, p.side)
    wrap(p, taps_ref, REACH, p.rows)
    hidden_rows(p, where, taps_ref, w_in, bias_in, act_ref, slope_ref, p.rows - 2, lambda s: s + REACH)


def outer_kernel(p, where, near, far, w_in, bias_in, _taps, _act, _slope, taps_ref, act_ref, slope_ref, rows_ref):
    fill_halo(p, where, near, far, rows_ref, taps_ref, False, p.side)
    wrap(p, taps_ref, 0, REACH)
    wrap(p, taps_ref, REACH + p.rows, REACH)
    edge = lambda s: jnp.where(s < REACH, s, s + p.rows - 2)
    hidden_rows(p, where, taps_ref, w_in, bias_in, act_ref, slope_ref, 2 * REACH, edge)


def score_kernel(p, which, where, *refs):
    n = p.n
    act_ref, w_out, bias_out = refs[:3]
    targets, wide_ref, resid_ref, parts = refs[3 : n + 3], refs[n + 3], refs[n + 4], refs[n + 5 :]
    me = where[0]
    pair = 1 - where[1] if which == 0 else where[1]
    wide_ref[...] = jnp.zeros_like(wide_ref)

    def score_row(step, carry):
        total = None
        for i in range(p.taps):
            a = act_ref[pair * REACH + step + i].reshape(p.total * p.wp, p.hidden)
            term = dot(a, w_out[i], True)
            total = term if total is None else total + term
        spread(p, total, parts)
        for d in range(n):
            for t in range(p.local):
                s = untap(p, parts, (me ^ d) * p.local + t, 8, p.wx, False) + bias_out[...]
                wide_ref[d, pl.ds(pl.multiple_of((step * p.local + t) * p.wx, 8), p.wx), :] = s
        return carry

    lax.fori_loop(0, REACH, score_row, 0)
    for d in range(n):
        for m in range(p.halfp // LANES):
            cols = slice(m * LANES, (m + 1) * LANES)
            tile = wide_ref[d, cols, :].T[: p.cp]
            target = targets[d][:, pl.ds(pl.multiple_of(pair * p.halfp + m * LANES, LANES), LANES)]
            resid_ref[d, :, cols] = (tile - jnp.log(target.astype(F32)) * (1.0 / CODE)).astype(BF16)


def gradient_rows(p, taps_ref, w_out, slope_ref, grad_ref, count, row_of):
    def body(step, carry):
        row = row_of(step)
        total = None
        for i in range(p.taps):
            a = taps_ref[row + 2 - i].reshape(p.total * p.wp, p.packed)
            term = dot(a, w_out[i], False)
            total = term if total is None else total + term
        grad = total.reshape(p.total, p.wp, p.hidden) * slope_ref[row]
        grad_ref[row, p.side : p.side + p.total] = grad.astype(BF16)
        return carry

    lax.fori_loop(0, count, body, 0)


def back_inner_kernel(p, where, *refs):
    n = p.n
    resid, wide, slope_ref, w_out = refs[:2], refs[2:4], refs[4], refs[5]
    taps_ref, grad_ref = refs[6:8]
    own_ref, scores = refs[8], refs[9 : n + 8]
    rows_ref, thin_ref = refs[n + 8 :]
    even = where[1] == 1
    fill_pairs(p, where, resid, rows_ref, taps_ref, True, REACH)
    fill_pairs(p, where, resid[::-1], rows_ref, taps_ref, True, 2 * REACH)
    gradient_rows(p, taps_ref, w_out, slope_ref, grad_ref, p.rows - 2, lambda s: s + REACH)
    wrap(p, grad_ref, REACH, p.rows - 2)
    for d in range(n):
        for r in range(p.rows):
            first, second = wide if r < REACH else wide[::-1]
            for t in range(p.local):
                start = p.at(r % REACH, t) + DEPTH
                at = (r * p.local + t) * p.wc
                here = slice(start, start + p.wc)
                thin_ref[at : at + p.wc, :] = jnp.where(even, first[d, here, :], second[d, here, :])
        turn(p, thin_ref, own_ref if d == 0 else scores[d - 1], 0)


def turn(p, thin_ref, out_ref, begin):
    for m in range(p.out // LANES):
        tile = thin_ref[m * LANES : (m + 1) * LANES, :].T[: p.cp]
        out_ref[:, begin + m * LANES : begin + (m + 1) * LANES] = tile.astype(out_ref.dtype)


def back_outer_kernel(p, where, near, far, slope_ref, w_out, _taps, _grad, taps_ref, grad_ref, rows_ref):
    fill_pairs(p, where, (far, near), rows_ref, taps_ref, True, 0)
    fill_pairs(p, where, (near, far), rows_ref, taps_ref, True, 3 * REACH)
    edge = lambda s: jnp.where(s < REACH, s, s + p.rows - 2)
    gradient_rows(p, taps_ref, w_out, slope_ref, grad_ref, 2 * REACH, edge)
    wrap(p, grad_ref, 0, REACH)
    wrap(p, grad_ref, p.rows, REACH)


def guide_kernel(p, d, where, grad_ref, w_in, *refs):
    out_ref, thin_ref, parts = refs[-4], refs[-3], refs[-2:]
    t0 = (where[0] ^ d) * p.local
    total = None
    for i in range(p.taps):
        for k in range(p.window):
            a = grad_ref[2 - i : 2 - i + p.rows, pl.ds(t0 + 2 * p.side - k, p.local)]
            a = a.reshape(p.rows * p.local * p.wp, p.hidden)
            term = dot(a, w_in[i * p.window + k], True)
            total = term if total is None else total + term
    spread(p, total, parts)
    for r in range(p.rows * p.local):
        thin_ref[r * p.wc : (r + 1) * p.wc, :] = untap(p, parts, r, 8 + DEPTH, p.wc, True)
    turn(p, thin_ref, out_ref, 0)
    if len(refs) > 4:
        out_ref[:, p.out :] = refs[0][...]


def join_kernel(p, begins, where, *refs):
    fields = len(begins)
    ins, outs, held = refs[: p.n * fields], refs[p.n * fields : -1], refs[-1]
    per = LANES // p.wc
    lane = lanes_of((p.chans, LANES))

    @pl.when(pl.program_id(0) == 0)
    def _():
        for f in range(fields):
            for d in range(p.n):
                block = ins[f * p.n + d][:, begins[f][d] : begins[f][d] + p.out]
                held[f, where[0] ^ d] = block.astype(F32)

    def join_state(t):
        for f in range(fields):
            for r in range(p.rows):
                start = (r * p.local + t) * p.wc
                base, off = start // LANES * LANES, start % LANES
                for m in range(p.lon // LANES):
                    tile = None
                    for u in range(per):
                        piece = held[f, m * per + u, : p.chans, base : base + LANES]
                        step = (u * p.wc - off) % LANES
                        if step:
                            piece = pltpu.roll(piece, step, 1)
                        tile = piece if tile is None else jnp.where(lane < u * p.wc, tile, piece)
                    outs[f][0, :, r, m * LANES : (m + 1) * LANES] = tile

    for t in range(p.local):
        pl.when(pl.program_id(0) == t)(functools.partial(join_state, t))


def send_tm(p, value, d):
    return lax.ppermute(value, "tm", [(i, i ^ d) for i in range(p.n)])


def relay_tm(p, blocks, bit):
    moving = [d for d in range(p.n) if d & bit]
    moved = send_tm(p, jnp.stack([blocks[d] for d in moving]), bit)
    blocks = list(blocks)
    for at, d in enumerate(moving):
        blocks[d] = moved[at]
    return blocks


def send_near(p, value):
    return lax.ppermute(value, "lat", [(i, i ^ 1) for i in range(p.m)])


def send_far(p, value):
    return lax.ppermute(value, "lat", [(i, ((i + 1) ^ 1) - 1) for i in range(1, p.m - 1)])


def shards(states, observed, conv_in, bias_in, conv_out, bias_out):
    p = Plan(states, conv_in)
    n = p.n
    even = lax.axis_index("lat") % 2 == 0
    sds = jax.ShapeDtypeStruct
    kernel = functools.partial
    scratch = pltpu.VMEM

    def split(field, place, coded, width):
        shape = [sds((p.cp, width), BF16)] * n
        held = [scratch((n, p.cp, width), F32)]
        return call(
            kernel(split_kernel, p, place, coded), shape, held, [field], 8 << 20, 1.5, states=p.local, ins_by=True
        )

    mine = split(states, p.at, False, p.posp)
    blocks = [mine[0]]
    for d in range(1, n):
        blocks.append(send_tm(p, mine[d], d))
    w_in, w_out = call(
        kernel(weights_kernel, p),
        [sds((p.taps * p.window, p.packed, p.hidden), BF16), sds((p.taps, p.packed, p.hidden), BF16)],
        [scratch((p.taps, up(p.window * p.chans, 8), p.hidden), F32), scratch((p.window + 1, p.packed, p.hidden), F32)],
        [jnp.swapaxes(conv_in, 2, 3), conv_out],
        16 << 20, 2,
    )
    goal = split(observed, p.paired, True, 2 * p.halfp)
    stages = [1 << b for b in range(n.bit_length() - 1)]
    goals = relay_tm(p, goal, stages[0])
    b_in = bias_in.reshape(1, p.hidden)
    b_out = jnp.pad(bias_out, (0, LANES - p.chans)).reshape(1, LANES)
    low = jnp.stack([b[:, : p.msg] for b in blocks])
    high = jnp.stack([b[:, p.cut :] for b in blocks])
    near = send_near(p, jnp.where(even, high, low))
    far = send_far(p, jnp.where(even, low, high))

    columns = scratch((p.posp + 32, LANES), F32)
    deep = p.rows + 2 * REACH
    around = p.total + 2 * p.side
    taps_shape = sds((deep, around, p.wp, p.packed), BF16)
    act_shape = sds((p.rows + 2, p.total, p.wp, p.hidden), BF16)
    slope_shape = sds((p.rows + 2, p.total, p.wp, p.hidden), F32)
    taps = call(kernel(early_kernel, p), [taps_shape], [columns], blocks[:-1], 16 << 20, 1)[0]
    inner = call(
        kernel(inner_kernel, p), [taps_shape, act_shape, slope_shape], [columns],
        [blocks[-1], w_in, b_in, taps], 24 << 20, 5, {3: 0},
    )
    for bit in stages[1:]:
        goals = relay_tm(p, goals, bit)
    _, act, slope = call(
        kernel(outer_kernel, p), [taps_shape, act_shape, slope_shape], [columns],
        [near, far, w_in, b_in, *inner], 24 << 20, 8, {4: 0, 5: 1, 6: 2},
    )
    part = [scratch((p.total, p.wp + 16, LANES), F32)] * 2

    def score(which):
        return call(
            kernel(score_kernel, p, which),
            [sds((n, p.halfp, LANES), F32), sds((n, p.cp, p.halfp), BF16)], part,
            [act, w_out, b_out, *goals], 24 << 20, 2,
        )

    wide_far, resid_far = score(0)
    far = send_far(p, resid_far)
    wide_near, resid_near = score(1)
    near = send_near(p, resid_near)
    taps_shape = sds((deep, p.total, p.wp, p.packed), BF16)
    grad_shape = sds((p.rows + 2, around, p.wp, p.hidden), BF16)
    thin = sds((p.cp, p.out), BF16)
    thin_rows = scratch((p.out, LANES), F32)
    out = call(
        kernel(back_inner_kernel, p),
        [taps_shape, grad_shape, sds((p.cp, p.out), F32)] + [thin] * (n - 1),
        [columns, thin_rows],
        [resid_far, resid_near, wide_far, wide_near, slope, w_out], 32 << 20, 2.3,
    )
    taps, grad, scores = out[0], out[1], list(out[2:])
    scores[1] = send_tm(p, scores[1], 1)
    taps, grad = call(
        kernel(back_outer_kernel, p), [taps_shape, grad_shape], [columns],
        [near, far, slope, w_out, taps, grad], 24 << 20, 3, {4: 0, 5: 1},
    )
    parts = [None] * n
    for d in [*range(n - 1, 0, -1), 0]:
        part = [scratch((p.rows * p.local, p.wp + 16, LANES), F32)] * 2
        ride = [scores[d]] if d > 1 else []
        shape = sds((p.cp, (1 + len(ride)) * p.out), BF16 if d else F32)
        parts[d] = call(
            kernel(guide_kernel, p, d), [shape], [thin_rows, *part],
            [grad, w_in, *ride], 16 << 20, 2,
        )[0]
        if d:
            parts[d] = send_tm(p, parts[d], d)

    begins = [[0, 0] + [p.out] * (n - 2), [0] * n]
    shape = [sds((p.local, p.chans, p.rows, p.lon), F32)] * 2
    held = [scratch((2, n, p.cp, p.out), F32)]
    return tuple(
        call(
            kernel(join_kernel, p, begins), shape, held, scores[:2] + parts[2:] + parts, 16 << 20, 1.5,
            states=p.local, outs_by=True,
        )
    )


def solution(mesh):
    in_specs = (P("tm", None, "lat", None), P("tm", None, "lat", None), P(), P(), P(), P())
    out_specs = (P("tm", None, "lat", None), P("tm", None, "lat", None))
    return jax.shard_map(shards, mesh=mesh, in_specs=in_specs, out_specs=out_specs, check_vma=False)
```

```python
import functools

import jax
import jax.numpy as jnp
from jax import lax
from jax.experimental import pallas as pl
from jax.experimental.pallas import tpu as pltpu
from jax.sharding import PartitionSpec as P


F32 = jnp.float32
BF16 = jnp.bfloat16
LANES = 128
DEPTH = 4
REACH = 2
CODE = 14.0
VMEM = pl.BlockSpec(memory_space=pltpu.VMEM)


def up(value, step):
    return -(-value // step) * step


class Plan:
    def __init__(self, states, conv_in):
        self.n = lax.axis_size("tm")
        self.m = lax.axis_size("lat")
        self.local, self.chans, self.rows, self.lon = states.shape
        self.taps = conv_in.shape[0]
        self.hidden = conv_in.shape[2]
        self.window = conv_in.shape[3] // self.chans
        self.side = self.window // 2
        self.total = self.local * self.n
        self.wc = self.lon // self.n
        self.wx = self.wc + 2 * DEPTH
        self.wp = up(self.wx, 16)
        self.cp = up(self.chans, 8)
        self.packed = 2 * LANES
        self.pos = self.rows * self.local * self.wx
        self.posp = up(self.pos, LANES)
        self.half = REACH * self.local * self.wx
        self.cut = (self.pos - self.half) // LANES * LANES
        self.msg = max(self.posp - self.cut, up(self.half, LANES))
        self.cut = self.posp - self.msg
        self.shift = self.pos - self.half - self.cut
        self.halfp = up(self.half, LANES)
        self.out = self.rows * self.local * self.wc
        assert self.taps == 3 and LANES <= 2 * self.chans and 3 * self.chans <= self.packed
        assert self.out % LANES == 0 and LANES % self.wc == 0 and self.wx % 8 == 0
        assert self.lon % LANES == 0 and self.rows == 2 * REACH and self.n & (self.n - 1) == 0

    def at(self, row, t):
        return (row * self.local + t) * self.wx

    def paired(self, row, t):
        return row // REACH * self.halfp + self.at(row % REACH, t)


def here():
    row = lax.axis_index("lat")
    flags = [row % 2 == 0, row == 0, row == lax.axis_size("lat") - 1]
    return [lax.axis_index("tm")] + [flag.astype(jnp.int32) for flag in flags]


def call(kernel, outs, scratch, args, limit, microseconds, aliases={}, states=0, ins_by=False, outs_by=False):
    def one(shape):
        return pl.BlockSpec((1,) + tuple(shape[1:]), lambda t: (t,) + (0,) * (len(shape) - 1))

    return pl.pallas_call(
        lambda *refs: kernel(here(), *refs),
        grid=(states,) if states else (),
        out_shape=outs,
        in_specs=[one(a.shape) if ins_by else VMEM for a in args],
        out_specs=[one(a.shape) if outs_by else VMEM for a in outs],
        scratch_shapes=scratch,
        input_output_aliases=aliases,
        compiler_params=pltpu.CompilerParams(vmem_limit_bytes=limit),
        cost_estimate=pl.CostEstimate(flops=int(microseconds * 1e9), bytes_accessed=0, transcendentals=0),
    )(*args)


def lanes_of(shape):
    return lax.broadcasted_iota(jnp.int32, shape, len(shape) - 1)


def split_kernel(p, place, coded, where, x_ref, *refs):
    outs, held = refs[: p.n], refs[p.n]

    @pl.when(pl.program_id(0) == 0)
    def _():
        held[...] = jnp.zeros_like(held)

    def place_state(t):
        for r in range(p.rows):
            v = x_ref[0, :, r, :]
            start = place(r, t)
            base, off = start // LANES * LANES, start % LANES
            width = LANES if off + p.wx <= LANES else 2 * LANES
            lane = lanes_of((p.chans, width))
            inside = (lane >= off) & (lane < off + p.wx)
            for q in range(p.n):
                y = pltpu.roll(v, (off + DEPTH - p.wc * q) % p.lon, 1)[:, :width]
                old = held[q, : p.chans, base : base + width]
                held[q, : p.chans, base : base + width] = jnp.where(inside, y, old)

    for t in range(p.local):
        pl.when(pl.program_id(0) == t)(functools.partial(place_state, t))

    @pl.when(pl.program_id(0) == p.local - 1)
    def _():
        for d in range(p.n):
            block = held[where[0] ^ d]
            outs[d][...] = (jnp.exp(CODE * block) if coded else block).astype(BF16)


def weights_kernel(p, where, k_in, k_out, w_in, w_out, flat_ref, held):
    held[...] = jnp.zeros_like(held)
    c = p.chans
    for i in range(p.taps):
        for j in range(p.taps):
            flat_ref[j, : p.window * c] = k_in[i, j].astype(F32)
        for k in range(p.window):
            for j in range(p.taps):
                held[k, j * c : (j + 1) * c, :] = flat_ref[j, k * c : (k + 1) * c, :]
            w_in[i * p.window + k] = held[k].astype(BF16)
        for j in range(p.taps):
            held[p.window, j * c : (j + 1) * c, :] = k_out[i, j].astype(F32)
        w_out[i] = held[p.window].astype(BF16)


def to_columns(block, rows_ref):
    depth, width = block.shape
    for m in range(width // LANES):
        tile = block[:, m * LANES : (m + 1) * LANES]
        tile = jnp.concatenate([tile, jnp.zeros((LANES - depth, LANES), BF16)], axis=0)
        rows_ref[8 + m * LANES : 8 + (m + 1) * LANES, :] = tile.T.astype(F32)


def taps_of(p, rows_ref, start, flip):
    v = [rows_ref[8 + start + j : 8 + start + j + p.wp, :].astype(BF16) for j in (-1, 0, 1)]
    if flip:
        v = v[::-1]
    lane = lanes_of((p.wp, LANES))
    middle = pltpu.roll(v[1], p.chans, 1)
    low = jnp.where(lane < p.chans, v[0], middle)
    high = jnp.where(lane < 2 * p.chans - LANES, middle, pltpu.roll(v[2], 2 * p.chans - LANES, 1))
    return jnp.concatenate([low, high], axis=1)


def spread(p, total, parts):
    lead = total.shape[0] // p.wp
    for tile, ref in enumerate(parts):
        ref[:, 8 : 8 + p.wp, :] = total[:, tile * LANES : (tile + 1) * LANES].reshape(lead, p.wp, LANES)


def untap(p, parts, lead, start, count, flip):
    before, after = (1, -1) if flip else (-1, 1)
    first = parts[0][lead, start + before : start + before + count, :]
    low = pltpu.roll(parts[0][lead, start : start + count, :], LANES - p.chans, 1)
    high = pltpu.roll(parts[1][lead, start : start + count, :], LANES - p.chans, 1)
    lane = lanes_of((count, LANES))
    middle = jnp.where(lane < LANES - p.chans, low, high)
    last = pltpu.roll(parts[1][lead, start + after : start + after + count, :], 2 * LANES - 2 * p.chans, 1)
    return jnp.where(lane < p.chans, first + middle + last, 0.0)


def fill_own(p, where, blocks, rows_ref, taps_ref, flip, base):
    me = where[0]
    for d, block in blocks.items():
        t0 = (me ^ d) * p.local + base
        to_columns(block[...], rows_ref)
        for r in range(p.rows):
            for t in range(p.local):
                taps_ref[r, t0 + t] = taps_of(p, rows_ref, p.at(r, t), flip)


def fill_halo(p, where, blocks, begin, rows_ref, taps_ref):
    me, even = where[0], where[1] == 1
    for d in range(p.n):
        t0 = (me ^ d) * p.local + p.side
        to_columns(jnp.where(even, blocks[0][d], blocks[1][d]), rows_ref)
        for r in range(REACH):
            for t in range(p.local):
                taps_ref[r, t0 + t] = taps_of(p, rows_ref, begin + p.at(r, t), False)
    wrap(p, taps_ref, 0, REACH)


def fill_pairs(p, where, halves, rows_ref, taps_ref, flip, row):
    me, even = where[0], where[1] == 1
    for d in range(p.n):
        to_columns(jnp.where(even, halves[0][d], halves[1][d]), rows_ref)
        for r in range(REACH):
            for t in range(p.local):
                taps_ref[row + r, (me ^ d) * p.local + t] = taps_of(p, rows_ref, p.at(r, t), flip)


def wrap(p, ref, begin, count):
    for row in range(begin, begin + count):
        for e in range(p.side):
            ref[row, e] = ref[row, p.total + e]
            ref[row, p.total + p.side + e] = ref[row, p.side + e]


def row_mask(p, where, row):
    outside = ((row == 0) & (where[2] == 1)) | ((row == p.rows + 1) & (where[3] == 1))
    return jnp.where(outside, 0.0, 1.0)


def dot(a, b, transposed):
    dims = (((1,), (1 if transposed else 0,)), ((), ()))
    return lax.dot_general(a, b, dims, preferred_element_type=F32)


def hidden_row(p, where, row, taps, w_in, bias_in, act_ref, slope_ref):
    total = None
    for i in range(p.taps):
        ref, at = taps[i]
        for k in range(p.window):
            a = ref[at, k : k + p.total].reshape(p.total * p.wp, p.packed)
            term = dot(a, w_in[i * p.window + k], False)
            total = term if total is None else total + term
    pre = total + bias_in[...]
    sig = 0.5 * jnp.tanh(0.5 * pre) + 0.5
    act = pre * sig
    slope = sig + act * (1.0 - sig)
    mask = row_mask(p, where, row)
    act_ref[row] = (act * mask).astype(BF16).reshape(p.total, p.wp, p.hidden)
    slope_ref[row] = (slope * mask).reshape(p.total, p.wp, p.hidden)


def early_kernel(p, where, *refs):
    blocks, taps_ref, rows_ref = refs[: p.n - 1], refs[p.n - 1], refs[p.n]
    fill_own(p, where, dict(enumerate(blocks)), rows_ref, taps_ref, False, p.side)


def inner_kernel(p, where, block, w_in, bias_in, _taps, taps_ref, act_ref, slope_ref, rows_ref):
    fill_own(p, where, {p.n - 1: block}, rows_ref, taps_ref, False, p.side)
    wrap(p, taps_ref, 0, p.rows)

    for step in range(p.rows - 2):
        taps = [(taps_ref, step + i) for i in range(p.taps)]
        hidden_row(p, where, step + REACH, taps, w_in, bias_in, act_ref, slope_ref)


def outer_kernel(p, where, near, far, w_in, bias_in, taps_ref, _act, _slope, act_ref, slope_ref, *scratch):
    below, above, rows_below, rows_above = scratch

    def row_at(row):
        taps = []
        for at in range(row - REACH, row - REACH + p.taps):
            ref = below if at < 0 else above if at >= p.rows else taps_ref
            taps.append((ref, at % p.rows if ref is above else at + REACH if ref is below else at))
        hidden_row(p, where, row, taps, w_in, bias_in, act_ref, slope_ref)

    fill_halo(p, where, (far, near), p.shift, rows_below, below)
    row_at(1)
    fill_halo(p, where, (near, far), 0, rows_above, above)
    row_at(0)
    row_at(p.rows)
    row_at(p.rows + 1)


def score_kernel(p, which, where, *refs):
    n = p.n
    act_ref, w_out, bias_out = refs[:3]
    targets, wide_ref, resid_ref, parts = refs[3 : n + 3], refs[n + 3], refs[n + 4], refs[n + 5 :]
    me = where[0]
    pair = 1 - where[1] if which == 0 else where[1]
    for d in range(n):
        wide_ref[d, p.half :, :] = jnp.zeros((p.halfp - p.half, LANES), F32)
    for step in range(REACH):
        total = None
        for i in range(p.taps):
            a = act_ref[pair * REACH + step + i].reshape(p.total * p.wp, p.hidden)
            term = dot(a, w_out[i], True)
            total = term if total is None else total + term
        here = parts[2 * step : 2 * step + 2]
        spread(p, total, here)
        for d in range(n):
            for t in range(p.local):
                s = untap(p, here, (me ^ d) * p.local + t, 8, p.wx, False) + bias_out[...]
                wide_ref[d, p.at(step, t) : p.at(step, t) + p.wx, :] = s
    for d in range(n):
        for m in range(p.halfp // LANES):
            cols = slice(m * LANES, (m + 1) * LANES)
            tile = wide_ref[d, cols, :].T[: p.cp]
            target = targets[d][:, pl.ds(pl.multiple_of(pair * p.halfp + m * LANES, LANES), LANES)]
            resid_ref[d, :, cols] = (tile - jnp.log(target.astype(F32)) * (1.0 / CODE)).astype(BF16)


def gradient_row(p, row, taps, w_out, slope_ref, grad_ref):
    total = None
    for i in range(p.taps):
        ref, at = taps[i]
        term = dot(ref[at].reshape(p.total * p.wp, p.packed), w_out[i], False)
        total = term if total is None else total + term
    grad = total.reshape(p.total, p.wp, p.hidden) * slope_ref[row]
    grad_ref[row, p.side : p.side + p.total] = grad.astype(BF16)
    wrap(p, grad_ref, row, 1)


def back_inner_kernel(p, where, *refs):
    n = p.n
    resid, wide, slope_ref, w_out = refs[:2], refs[2:4], refs[4], refs[5]
    taps_ref, grad_ref = refs[6:8]
    own_ref, scores = refs[8], refs[9 : n + 8]
    rows_ref, thin_ref = refs[n + 8 :]
    even = where[1] == 1
    fill_pairs(p, where, resid, rows_ref, taps_ref, True, 0)
    fill_pairs(p, where, resid[::-1], rows_ref, taps_ref, True, REACH)
    for row in range(REACH, p.rows):
        taps = [(taps_ref, row - i) for i in range(p.taps)]
        gradient_row(p, row, taps, w_out, slope_ref, grad_ref)
    for d in range(n):
        for r in range(p.rows):
            first, second = wide if r < REACH else wide[::-1]
            for t in range(p.local):
                start = p.at(r % REACH, t) + DEPTH
                at = (r * p.local + t) * p.wc
                here = slice(start, start + p.wc)
                thin_ref[at : at + p.wc, :] = jnp.where(even, first[d, here, :], second[d, here, :])
        turn(p, thin_ref, own_ref if d == 0 else scores[d - 1], 0)


def back_outer_kernel(p, where, near, far, slope_ref, w_out, taps_ref, _grad, grad_ref, *scratch):
    below, above, rows_below, rows_above = scratch

    def row_at(row):
        taps = []
        for at in range(row, row - p.taps, -1):
            ref = below if at < 0 else above if at >= p.rows else taps_ref
            taps.append((ref, at % p.rows if ref is above else at + REACH if ref is below else at))
        gradient_row(p, row, taps, w_out, slope_ref, grad_ref)

    fill_pairs(p, where, (far, near), rows_below, below, True, 0)
    row_at(1)
    fill_pairs(p, where, (near, far), rows_above, above, True, 0)
    row_at(0)
    row_at(p.rows)
    row_at(p.rows + 1)


def turn(p, thin_ref, out_ref, begin):
    for m in range(p.out // LANES):
        tile = thin_ref[m * LANES : (m + 1) * LANES, :].T[: p.cp]
        out_ref[:, begin + m * LANES : begin + (m + 1) * LANES] = tile.astype(out_ref.dtype)


def guide_kernel(p, d, where, grad_ref, w_in, *refs):
    out_ref, thin_ref, parts = refs[-4], refs[-3], refs[-2:]
    t0 = (where[0] ^ d) * p.local
    total = None
    for i in range(p.taps):
        for k in range(p.window):
            a = grad_ref[2 - i : 2 - i + p.rows, pl.ds(t0 + 2 * p.side - k, p.local)]
            a = a.reshape(p.rows * p.local * p.wp, p.hidden)
            term = dot(a, w_in[i * p.window + k], True)
            total = term if total is None else total + term
    spread(p, total, parts)
    for r in range(p.rows * p.local):
        thin_ref[r * p.wc : (r + 1) * p.wc, :] = untap(p, parts, r, 8 + DEPTH, p.wc, True)
    turn(p, thin_ref, out_ref, 0)
    if len(refs) > 4:
        out_ref[:, p.out :] = refs[0][...]


def join_kernel(p, begins, where, *refs):
    fields = len(begins)
    ins, outs, held = refs[: p.n * fields], refs[p.n * fields : -1], refs[-1]
    per = LANES // p.wc
    lane = lanes_of((p.chans, LANES))

    @pl.when(pl.program_id(0) == 0)
    def _():
        for f in range(fields):
            for d in range(p.n):
                block = ins[f * p.n + d][:, begins[f][d] : begins[f][d] + p.out]
                held[f, where[0] ^ d] = block.astype(F32)

    def join_state(t):
        for f in range(fields):
            for r in range(p.rows):
                start = (r * p.local + t) * p.wc
                base, off = start // LANES * LANES, start % LANES
                for m in range(p.lon // LANES):
                    tile = None
                    for u in range(per):
                        piece = held[f, m * per + u, : p.chans, base : base + LANES]
                        step = (u * p.wc - off) % LANES
                        if step:
                            piece = pltpu.roll(piece, step, 1)
                        tile = piece if tile is None else jnp.where(lane < u * p.wc, tile, piece)
                    outs[f][0, :, r, m * LANES : (m + 1) * LANES] = tile

    for t in range(p.local):
        pl.when(pl.program_id(0) == t)(functools.partial(join_state, t))


def send_tm(p, value, d):
    return lax.ppermute(value, "tm", [(i, i ^ d) for i in range(p.n)])


def relay_tm(p, blocks, bit):
    moving = [d for d in range(p.n) if d & bit]
    moved = send_tm(p, jnp.stack([blocks[d] for d in moving]), bit)
    blocks = list(blocks)
    for at, d in enumerate(moving):
        blocks[d] = moved[at]
    return blocks


def send_near(p, value):
    return lax.ppermute(value, "lat", [(i, i ^ 1) for i in range(p.m)])


def send_far(p, value):
    return lax.ppermute(value, "lat", [(i, ((i + 1) ^ 1) - 1) for i in range(1, p.m - 1)])


def shards(states, observed, conv_in, bias_in, conv_out, bias_out):
    p = Plan(states, conv_in)
    n = p.n
    even = lax.axis_index("lat") % 2 == 0
    sds = jax.ShapeDtypeStruct
    kernel = functools.partial
    scratch = pltpu.VMEM

    def split(field, place, coded, width):
        shape = [sds((p.cp, width), BF16)] * n
        held = [scratch((n, p.cp, width), F32)]
        return call(
            kernel(split_kernel, p, place, coded), shape, held, [field], 8 << 20, 1.5, states=p.local, ins_by=True
        )

    mine = split(states, p.at, False, p.posp)
    blocks = [mine[0]]
    for d in range(1, n):
        blocks.append(send_tm(p, mine[d], d))
    w_in, w_out = call(
        kernel(weights_kernel, p),
        [sds((p.taps * p.window, p.packed, p.hidden), BF16), sds((p.taps, p.packed, p.hidden), BF16)],
        [scratch((p.taps, up(p.window * p.chans, 8), p.hidden), F32), scratch((p.window + 1, p.packed, p.hidden), F32)],
        [jnp.swapaxes(conv_in, 2, 3), conv_out],
        16 << 20, 2,
    )
    goal = split(observed, p.paired, True, 2 * p.halfp)
    stages = [1 << b for b in range(n.bit_length() - 1)]
    goals = relay_tm(p, goal, stages[0])
    b_in = bias_in.reshape(1, p.hidden)
    b_out = jnp.pad(bias_out, (0, LANES - p.chans)).reshape(1, LANES)
    low = jnp.stack([b[:, : p.msg] for b in blocks])
    high = jnp.stack([b[:, p.cut :] for b in blocks])
    near = send_near(p, jnp.where(even, high, low))
    far = send_far(p, jnp.where(even, low, high))

    columns = scratch((p.posp + 32, LANES), F32)
    around = p.total + 2 * p.side
    taps_shape = sds((p.rows, around, p.wp, p.packed), BF16)
    act_shape = sds((p.rows + 2, p.total, p.wp, p.hidden), BF16)
    slope_shape = sds((p.rows + 2, p.total, p.wp, p.hidden), F32)
    taps = call(kernel(early_kernel, p), [taps_shape], [columns], blocks[:-1], 16 << 20, 1)[0]
    inner = call(
        kernel(inner_kernel, p), [taps_shape, act_shape, slope_shape], [columns],
        [blocks[-1], w_in, b_in, taps], 24 << 20, 5, {3: 0},
    )
    for bit in stages[1:]:
        goals = relay_tm(p, goals, bit)
    edge = scratch((REACH, around, p.wp, p.packed), BF16)
    act, slope = call(
        kernel(outer_kernel, p), [act_shape, slope_shape], [edge, edge, columns, columns],
        [near, far, w_in, b_in, *inner], 24 << 20, 7, {5: 0, 6: 1},
    )
    part = [scratch((p.total, p.wp + 16, LANES), F32)] * (2 * REACH)

    def score(which):
        return call(
            kernel(score_kernel, p, which),
            [sds((n, p.halfp, LANES), F32), sds((n, p.cp, p.halfp), BF16)], part,
            [act, w_out, b_out, *goals], 24 << 20, 2,
        )

    wide_far, resid_far = score(0)
    far = send_far(p, resid_far)
    wide_near, resid_near = score(1)
    near = send_near(p, resid_near)
    taps_shape = sds((p.rows, p.total, p.wp, p.packed), BF16)
    grad_shape = sds((p.rows + 2, around, p.wp, p.hidden), BF16)
    thin = sds((p.cp, p.out), BF16)
    thin_rows = scratch((p.out, LANES), F32)
    out = call(
        kernel(back_inner_kernel, p),
        [taps_shape, grad_shape, sds((p.cp, p.out), F32)] + [thin] * (n - 1),
        [columns, thin_rows],
        [resid_far, resid_near, wide_far, wide_near, slope, w_out], 32 << 20, 2.3,
    )
    taps, grad, scores = out[0], out[1], list(out[2:])
    scores[1] = send_tm(p, scores[1], 1)
    edge = scratch((REACH, p.total, p.wp, p.packed), BF16)
    grad = call(
        kernel(back_outer_kernel, p), [grad_shape], [edge, edge, columns, columns],
        [near, far, slope, w_out, taps, grad], 24 << 20, 2, {5: 0},
    )[0]
    parts = [None] * n
    for d in [*range(n - 1, 0, -1), 0]:
        part = [scratch((p.rows * p.local, p.wp + 16, LANES), F32)] * 2
        ride = [scores[d]] if d > 1 else []
        shape = sds((p.cp, (1 + len(ride)) * p.out), BF16 if d else F32)
        parts[d] = call(
            kernel(guide_kernel, p, d), [shape], [thin_rows, *part],
            [grad, w_in, *ride], 16 << 20, 2,
        )[0]
        if d:
            parts[d] = send_tm(p, parts[d], d)

    def join(blocks, begins):
        shape = [sds((p.local, p.chans, p.rows, p.lon), F32)]
        held = [scratch((1, n, p.cp, p.out), F32)]
        return call(kernel(join_kernel, p, [begins]), shape, held, blocks, 8 << 20, 1, states=p.local, outs_by=True)[0]

    begins = [0, 0] + [p.out] * (n - 2)
    return join(scores[:2] + parts[2:], begins), join(parts, [0] * n)


def solution(mesh):
    in_specs = (P("tm", None, "lat", None), P("tm", None, "lat", None), P(), P(), P(), P())
    out_specs = (P("tm", None, "lat", None), P("tm", None, "lat", None))
    return jax.shard_map(shards, mesh=mesh, in_specs=in_specs, out_specs=out_specs, check_vma=False)
```

```python
import functools

import jax
import jax.numpy as jnp
from jax import lax
from jax.experimental import pallas as pl
from jax.experimental.pallas import tpu as pltpu
from jax.sharding import PartitionSpec as P


F32 = jnp.float32
BF16 = jnp.bfloat16
LANES = 128
DEPTH = 4
REACH = 2
CODE = 14.0
VMEM = pl.BlockSpec(memory_space=pltpu.VMEM)


def up(value, step):
    return -(-value // step) * step


class Plan:
    def __init__(self, states, conv_in):
        self.n = lax.axis_size("tm")
        self.m = lax.axis_size("lat")
        self.local, self.chans, self.rows, self.lon = states.shape
        self.taps = conv_in.shape[0]
        self.hidden = conv_in.shape[2]
        self.window = conv_in.shape[3] // self.chans
        self.side = self.window // 2
        self.total = self.local * self.n
        self.wc = self.lon // self.n
        self.wx = self.wc + 2 * DEPTH
        self.wp = up(self.wx, 16)
        self.cp = up(self.chans, 8)
        self.packed = 2 * LANES
        self.pos = self.rows * self.local * self.wx
        self.posp = up(self.pos, LANES)
        self.half = REACH * self.local * self.wx
        self.cut = (self.pos - self.half) // LANES * LANES
        self.msg = max(self.posp - self.cut, up(self.half, LANES))
        self.cut = self.posp - self.msg
        self.shift = self.pos - self.half - self.cut
        self.halfp = up(self.half, LANES)
        self.out = self.rows * self.local * self.wc
        assert self.taps == 3 and LANES <= 2 * self.chans and 3 * self.chans <= self.packed
        assert self.out % LANES == 0 and LANES % self.wc == 0 and self.wx % 8 == 0
        assert self.lon % LANES == 0 and self.rows == 2 * REACH and self.n & (self.n - 1) == 0

    def at(self, row, t):
        return (row * self.local + t) * self.wx

    def paired(self, row, t):
        return row // REACH * self.halfp + self.at(row % REACH, t)


def here():
    row = lax.axis_index("lat")
    flags = [row % 2 == 0, row == 0, row == lax.axis_size("lat") - 1]
    return [lax.axis_index("tm")] + [flag.astype(jnp.int32) for flag in flags]


def call(kernel, outs, scratch, args, limit, microseconds, aliases={}, states=0, ins_by=False, outs_by=False):
    def one(shape):
        return pl.BlockSpec((1,) + tuple(shape[1:]), lambda t: (t,) + (0,) * (len(shape) - 1))

    return pl.pallas_call(
        lambda *refs: kernel(here(), *refs),
        grid=(states,) if states else (),
        out_shape=outs,
        in_specs=[one(a.shape) if ins_by else VMEM for a in args],
        out_specs=[one(a.shape) if outs_by else VMEM for a in outs],
        scratch_shapes=scratch,
        input_output_aliases=aliases,
        compiler_params=pltpu.CompilerParams(vmem_limit_bytes=limit),
        cost_estimate=pl.CostEstimate(flops=int(microseconds * 1e9), bytes_accessed=0, transcendentals=0),
    )(*args)


def lanes_of(shape):
    return lax.broadcasted_iota(jnp.int32, shape, len(shape) - 1)


def split_kernel(p, place, coded, where, x_ref, *refs):
    outs, held = refs[: p.n], refs[p.n]

    @pl.when(pl.program_id(0) == 0)
    def _():
        held[...] = jnp.zeros_like(held)

    def place_state(t):
        for r in range(p.rows):
            v = x_ref[0, :, r, :]
            start = place(r, t)
            base, off = start // LANES * LANES, start % LANES
            width = LANES if off + p.wx <= LANES else 2 * LANES
            lane = lanes_of((p.chans, width))
            inside = (lane >= off) & (lane < off + p.wx)
            for q in range(p.n):
                y = pltpu.roll(v, (off + DEPTH - p.wc * q) % p.lon, 1)[:, :width]
                old = held[q, : p.chans, base : base + width]
                held[q, : p.chans, base : base + width] = jnp.where(inside, y, old)

    for t in range(p.local):
        pl.when(pl.program_id(0) == t)(functools.partial(place_state, t))

    @pl.when(pl.program_id(0) == p.local - 1)
    def _():
        for d in range(p.n):
            block = held[where[0] ^ d]
            outs[d][...] = (jnp.exp(CODE * block) if coded else block).astype(BF16)


def weights_kernel(p, where, k_in, k_out, w_in, w_out, flat_ref, held):
    held[...] = jnp.zeros_like(held)
    c = p.chans
    for i in range(p.taps):
        for j in range(p.taps):
            flat_ref[j, : p.window * c] = k_in[i, j].astype(F32)
        for k in range(p.window):
            for j in range(p.taps):
                held[k, j * c : (j + 1) * c, :] = flat_ref[j, k * c : (k + 1) * c, :]
            w_in[i * p.window + k] = held[k].astype(BF16)
        for j in range(p.taps):
            held[p.window, j * c : (j + 1) * c, :] = k_out[i, j].astype(F32)
        w_out[i] = held[p.window].astype(BF16)


def to_columns(block, rows_ref):
    depth, width = block.shape
    for m in range(width // LANES):
        tile = block[:, m * LANES : (m + 1) * LANES]
        tile = jnp.concatenate([tile, jnp.zeros((LANES - depth, LANES), BF16)], axis=0)
        rows_ref[8 + m * LANES : 8 + (m + 1) * LANES, :] = tile.T.astype(F32)


def taps_of(p, rows_ref, start, flip):
    v = [rows_ref[8 + start + j : 8 + start + j + p.wp, :].astype(BF16) for j in (-1, 0, 1)]
    if flip:
        v = v[::-1]
    lane = lanes_of((p.wp, LANES))
    middle = pltpu.roll(v[1], p.chans, 1)
    low = jnp.where(lane < p.chans, v[0], middle)
    high = jnp.where(lane < 2 * p.chans - LANES, middle, pltpu.roll(v[2], 2 * p.chans - LANES, 1))
    return jnp.concatenate([low, high], axis=1)


def spread(p, total, parts):
    lead = total.shape[0] // p.wp
    for tile, ref in enumerate(parts):
        ref[:, 8 : 8 + p.wp, :] = total[:, tile * LANES : (tile + 1) * LANES].reshape(lead, p.wp, LANES)


def untap(p, parts, lead, start, count, flip):
    before, after = (1, -1) if flip else (-1, 1)
    first = parts[0][lead, start + before : start + before + count, :]
    low = pltpu.roll(parts[0][lead, start : start + count, :], LANES - p.chans, 1)
    high = pltpu.roll(parts[1][lead, start : start + count, :], LANES - p.chans, 1)
    lane = lanes_of((count, LANES))
    middle = jnp.where(lane < LANES - p.chans, low, high)
    last = pltpu.roll(parts[1][lead, start + after : start + after + count, :], 2 * LANES - 2 * p.chans, 1)
    return jnp.where(lane < p.chans, first + middle + last, 0.0)


def fill_own(p, where, blocks, rows_ref, taps_ref, flip, base):
    me = where[0]
    for d, block in blocks.items():
        t0 = (me ^ d) * p.local + base
        to_columns(block[...], rows_ref)
        for r in range(p.rows):
            for t in range(p.local):
                taps_ref[r, t0 + t] = taps_of(p, rows_ref, p.at(r, t), flip)


def fill_halo(p, where, blocks, begin, rows_ref, taps_ref):
    me, even = where[0], where[1] == 1
    for d in range(p.n):
        t0 = (me ^ d) * p.local + p.side
        to_columns(jnp.where(even, blocks[0][d], blocks[1][d]), rows_ref)
        for r in range(REACH):
            for t in range(p.local):
                taps_ref[r, t0 + t] = taps_of(p, rows_ref, begin + p.at(r, t), False)
    wrap(p, taps_ref, 0, REACH)


def fill_pairs(p, where, halves, rows_ref, taps_ref, flip, row):
    me, even = where[0], where[1] == 1
    for d in range(p.n):
        to_columns(jnp.where(even, halves[0][d], halves[1][d]), rows_ref)
        for r in range(REACH):
            for t in range(p.local):
                taps_ref[row + r, (me ^ d) * p.local + t] = taps_of(p, rows_ref, p.at(r, t), flip)


def wrap(p, ref, begin, count):
    for row in range(begin, begin + count):
        for e in range(p.side):
            ref[row, e] = ref[row, p.total + e]
            ref[row, p.total + p.side + e] = ref[row, p.side + e]


def row_mask(p, where, row):
    outside = ((row == 0) & (where[2] == 1)) | ((row == p.rows + 1) & (where[3] == 1))
    return jnp.where(outside, 0.0, 1.0)


def dot(a, b, transposed):
    dims = (((1,), (1 if transposed else 0,)), ((), ()))
    return lax.dot_general(a, b, dims, preferred_element_type=F32)


def hidden_row(p, where, row, taps, w_in, bias_in, act_ref, slope_ref):
    total = None
    for i in range(p.taps):
        ref, at = taps[i]
        for k in range(p.window):
            a = ref[at, k : k + p.total].reshape(p.total * p.wp, p.packed)
            term = dot(a, w_in[i * p.window + k], False)
            total = term if total is None else total + term
    pre = total + bias_in[...]
    sig = 0.5 * jnp.tanh(0.5 * pre) + 0.5
    act = pre * sig
    slope = sig + act * (1.0 - sig)
    mask = row_mask(p, where, row)
    act_ref[row] = (act * mask).astype(BF16).reshape(p.total, p.wp, p.hidden)
    slope_ref[row] = (slope * mask).reshape(p.total, p.wp, p.hidden)


def early_kernel(p, where, *refs):
    blocks, taps_ref, rows_ref = refs[: p.n - 1], refs[p.n - 1], refs[p.n]
    fill_own(p, where, dict(enumerate(blocks)), rows_ref, taps_ref, False, p.side)


def inner_kernel(p, where, block, w_in, bias_in, _taps, taps_ref, act_ref, slope_ref, rows_ref):
    fill_own(p, where, {p.n - 1: block}, rows_ref, taps_ref, False, p.side)
    wrap(p, taps_ref, 0, p.rows)

    for step in range(p.rows - 2):
        taps = [(taps_ref, step + i) for i in range(p.taps)]
        hidden_row(p, where, step + REACH, taps, w_in, bias_in, act_ref, slope_ref)


def outer_kernel(p, where, near, far, w_in, bias_in, taps_ref, _act, _slope, act_ref, slope_ref, *scratch):
    below, above, rows_below, rows_above = scratch

    def row_at(row):
        taps = []
        for at in range(row - REACH, row - REACH + p.taps):
            ref = below if at < 0 else above if at >= p.rows else taps_ref
            taps.append((ref, at % p.rows if ref is above else at + REACH if ref is below else at))
        hidden_row(p, where, row, taps, w_in, bias_in, act_ref, slope_ref)

    fill_halo(p, where, (far, near), p.shift, rows_below, below)
    row_at(1)
    fill_halo(p, where, (near, far), 0, rows_above, above)
    row_at(0)
    row_at(p.rows)
    row_at(p.rows + 1)


def score_kernel(p, which, where, *refs):
    n = p.n
    act_ref, w_out, bias_out = refs[:3]
    targets, wide_ref, resid_ref, parts = refs[3 : n + 3], refs[n + 3], refs[n + 4], refs[n + 5 :]
    me = where[0]
    pair = 1 - where[1] if which == 0 else where[1]
    for d in range(n):
        wide_ref[d, p.half :, :] = jnp.zeros((p.halfp - p.half, LANES), F32)
    for step in range(REACH):
        total = None
        for i in range(p.taps):
            a = act_ref[pair * REACH + step + i].reshape(p.total * p.wp, p.hidden)
            term = dot(a, w_out[i], True)
            total = term if total is None else total + term
        here = parts[2 * step : 2 * step + 2]
        spread(p, total, here)
        for d in range(n):
            for t in range(p.local):
                s = untap(p, here, (me ^ d) * p.local + t, 8, p.wx, False) + bias_out[...]
                wide_ref[d, p.at(step, t) : p.at(step, t) + p.wx, :] = s
    for d in range(n):
        for m in range(p.halfp // LANES):
            cols = slice(m * LANES, (m + 1) * LANES)
            tile = wide_ref[d, cols, :].T[: p.cp]
            target = targets[d][:, pl.ds(pl.multiple_of(pair * p.halfp + m * LANES, LANES), LANES)]
            resid_ref[d, :, cols] = (tile - jnp.log(target.astype(F32)) * (1.0 / CODE)).astype(BF16)


def gradient_row(p, row, taps, w_out, slope_ref, grad_ref):
    total = None
    for i in range(p.taps):
        ref, at = taps[i]
        term = dot(ref[at].reshape(p.total * p.wp, p.packed), w_out[i], False)
        total = term if total is None else total + term
    grad = total.reshape(p.total, p.wp, p.hidden) * slope_ref[row]
    grad_ref[row, p.side : p.side + p.total] = grad.astype(BF16)
    wrap(p, grad_ref, row, 1)


def back_inner_kernel(p, where, *refs):
    n = p.n
    resid, wide, slope_ref, w_out = refs[:2], refs[2:4], refs[4], refs[5]
    taps_ref, grad_ref = refs[6:8]
    own_ref, scores = refs[8], refs[9 : n + 8]
    rows_ref, thin_ref = refs[n + 8 :]
    even = where[1] == 1
    fill_pairs(p, where, resid, rows_ref, taps_ref, True, 0)
    fill_pairs(p, where, resid[::-1], rows_ref, taps_ref, True, REACH)
    for row in range(REACH, p.rows):
        taps = [(taps_ref, row - i) for i in range(p.taps)]
        gradient_row(p, row, taps, w_out, slope_ref, grad_ref)
    for d in range(n):
        for r in range(p.rows):
            first, second = wide if r < REACH else wide[::-1]
            for t in range(p.local):
                start = p.at(r % REACH, t) + DEPTH
                at = (r * p.local + t) * p.wc
                here = slice(start, start + p.wc)
                thin_ref[at : at + p.wc, :] = jnp.where(even, first[d, here, :], second[d, here, :])
        turn(p, thin_ref, own_ref if d == 0 else scores[d - 1], 0)


def back_outer_kernel(p, where, near, far, slope_ref, w_out, taps_ref, _grad, grad_ref, *scratch):
    below, above, rows_below, rows_above = scratch

    def row_at(row):
        taps = []
        for at in range(row, row - p.taps, -1):
            ref = below if at < 0 else above if at >= p.rows else taps_ref
            taps.append((ref, at % p.rows if ref is above else at + REACH if ref is below else at))
        gradient_row(p, row, taps, w_out, slope_ref, grad_ref)

    fill_pairs(p, where, (far, near), rows_below, below, True, 0)
    row_at(1)
    fill_pairs(p, where, (near, far), rows_above, above, True, 0)
    row_at(0)
    row_at(p.rows)
    row_at(p.rows + 1)


def turn(p, thin_ref, out_ref, begin):
    for m in range(p.out // LANES):
        tile = thin_ref[m * LANES : (m + 1) * LANES, :].T[: p.cp]
        out_ref[:, begin + m * LANES : begin + (m + 1) * LANES] = tile.astype(out_ref.dtype)


def guide_kernel(p, d, where, grad_ref, w_in, *refs):
    out_ref, thin_ref, parts = refs[-4], refs[-3], refs[-2:]
    t0 = (where[0] ^ d) * p.local
    total = None
    for i in range(p.taps):
        for k in range(p.window):
            a = grad_ref[2 - i : 2 - i + p.rows, pl.ds(t0 + 2 * p.side - k, p.local)]
            a = a.reshape(p.rows * p.local * p.wp, p.hidden)
            term = dot(a, w_in[i * p.window + k], True)
            total = term if total is None else total + term
    spread(p, total, parts)
    for r in range(p.rows * p.local):
        thin_ref[r * p.wc : (r + 1) * p.wc, :] = untap(p, parts, r, 8 + DEPTH, p.wc, True)
    turn(p, thin_ref, out_ref, 0)
    if len(refs) > 4:
        out_ref[:, p.out :] = refs[0][...]


def join_kernel(p, begins, where, *refs):
    fields = len(begins)
    ins, outs, held = refs[: p.n * fields], refs[p.n * fields : -1], refs[-1]
    per = LANES // p.wc
    lane = lanes_of((p.chans, LANES))

    @pl.when(pl.program_id(0) == 0)
    def _():
        for f in range(fields):
            for d in range(p.n):
                block = ins[f * p.n + d][:, begins[f][d] : begins[f][d] + p.out]
                held[f, where[0] ^ d] = block.astype(F32)

    def join_state(t):
        for f in range(fields):
            for r in range(p.rows):
                start = (r * p.local + t) * p.wc
                base, off = start // LANES * LANES, start % LANES
                for m in range(p.lon // LANES):
                    tile = None
                    for u in range(per):
                        piece = held[f, m * per + u, : p.chans, base : base + LANES]
                        step = (u * p.wc - off) % LANES
                        if step:
                            piece = pltpu.roll(piece, step, 1)
                        tile = piece if tile is None else jnp.where(lane < u * p.wc, tile, piece)
                    outs[f][0, :, r, m * LANES : (m + 1) * LANES] = tile

    for t in range(p.local):
        pl.when(pl.program_id(0) == t)(functools.partial(join_state, t))


def send_tm(p, value, d):
    return lax.ppermute(value, "tm", [(i, i ^ d) for i in range(p.n)])


def relay_tm(p, blocks, bit):
    moving = [d for d in range(p.n) if d & bit]
    moved = send_tm(p, jnp.stack([blocks[d] for d in moving]), bit)
    blocks = list(blocks)
    for at, d in enumerate(moving):
        blocks[d] = moved[at]
    return blocks


def send_near(p, value):
    return lax.ppermute(value, "lat", [(i, i ^ 1) for i in range(p.m)])


def send_far(p, value):
    return lax.ppermute(value, "lat", [(i, ((i + 1) ^ 1) - 1) for i in range(1, p.m - 1)])


def shards(states, observed, conv_in, bias_in, conv_out, bias_out):
    p = Plan(states, conv_in)
    n = p.n
    even = lax.axis_index("lat") % 2 == 0
    sds = jax.ShapeDtypeStruct
    kernel = functools.partial
    scratch = pltpu.VMEM

    def split(field, place, coded, width):
        shape = [sds((p.cp, width), BF16)] * n
        held = [scratch((n, p.cp, width), F32)]
        return call(
            kernel(split_kernel, p, place, coded), shape, held, [pltpu.with_memory_space_constraint(field, pltpu.HBM)], 8 << 20, 1.5, states=p.local, ins_by=True
        )

    mine = split(states, p.at, False, p.posp)
    blocks = [mine[0]]
    for d in range(1, n):
        blocks.append(send_tm(p, mine[d], d))
    w_in, w_out = call(
        kernel(weights_kernel, p),
        [sds((p.taps * p.window, p.packed, p.hidden), BF16), sds((p.taps, p.packed, p.hidden), BF16)],
        [scratch((p.taps, up(p.window * p.chans, 8), p.hidden), F32), scratch((p.window + 1, p.packed, p.hidden), F32)],
        [jnp.swapaxes(conv_in, 2, 3), conv_out],
        16 << 20, 2,
    )
    goal = split(observed, p.paired, True, 2 * p.halfp)
    stages = [1 << b for b in range(n.bit_length() - 1)]
    goals = relay_tm(p, goal, stages[0])
    b_in = bias_in.reshape(1, p.hidden)
    b_out = jnp.pad(bias_out, (0, LANES - p.chans)).reshape(1, LANES)
    low = jnp.stack([b[:, : p.msg] for b in blocks])
    high = jnp.stack([b[:, p.cut :] for b in blocks])
    near = send_near(p, jnp.where(even, high, low))
    far = send_far(p, jnp.where(even, low, high))

    columns = scratch((p.posp + 32, LANES), F32)
    around = p.total + 2 * p.side
    taps_shape = sds((p.rows, around, p.wp, p.packed), BF16)
    act_shape = sds((p.rows + 2, p.total, p.wp, p.hidden), BF16)
    slope_shape = sds((p.rows + 2, p.total, p.wp, p.hidden), F32)
    taps = call(kernel(early_kernel, p), [taps_shape], [columns], blocks[:-1], 16 << 20, 1)[0]
    inner = call(
        kernel(inner_kernel, p), [taps_shape, act_shape, slope_shape], [columns],
        [blocks[-1], w_in, b_in, taps], 24 << 20, 5, {3: 0},
    )
    for bit in stages[1:]:
        goals = relay_tm(p, goals, bit)
    edge = scratch((REACH, around, p.wp, p.packed), BF16)
    act, slope = call(
        kernel(outer_kernel, p), [act_shape, slope_shape], [edge, edge, columns, columns],
        [near, far, w_in, b_in, *inner], 24 << 20, 7, {5: 0, 6: 1},
    )
    part = [scratch((p.total, p.wp + 16, LANES), F32)] * (2 * REACH)

    def score(which):
        return call(
            kernel(score_kernel, p, which),
            [sds((n, p.halfp, LANES), F32), sds((n, p.cp, p.halfp), BF16)], part,
            [act, w_out, b_out, *goals], 24 << 20, 2,
        )

    wide_far, resid_far = score(0)
    far = send_far(p, resid_far)
    wide_near, resid_near = score(1)
    near = send_near(p, resid_near)
    taps_shape = sds((p.rows, p.total, p.wp, p.packed), BF16)
    grad_shape = sds((p.rows + 2, around, p.wp, p.hidden), BF16)
    thin = sds((p.cp, p.out), BF16)
    thin_rows = scratch((p.out, LANES), F32)
    out = call(
        kernel(back_inner_kernel, p),
        [taps_shape, grad_shape, sds((p.cp, p.out), F32)] + [thin] * (n - 1),
        [columns, thin_rows],
        [resid_far, resid_near, wide_far, wide_near, slope, w_out], 32 << 20, 2.3,
    )
    taps, grad, scores = out[0], out[1], list(out[2:])
    scores[1] = send_tm(p, scores[1], 1)
    edge = scratch((REACH, p.total, p.wp, p.packed), BF16)
    grad = call(
        kernel(back_outer_kernel, p), [grad_shape], [edge, edge, columns, columns],
        [near, far, slope, w_out, taps, grad], 24 << 20, 2, {5: 0},
    )[0]
    parts = [None] * n
    for d in back_order(n):
        part = [scratch((p.rows * p.local, p.wp + 16, LANES), F32)] * 2
        ride = [scores[d]] if d > 1 else []
        shape = sds((p.cp, (1 + len(ride)) * p.out), BF16 if d else F32)
        parts[d] = call(
            kernel(guide_kernel, p, d), [shape], [thin_rows, *part],
            [grad, w_in, *ride], 16 << 20, 2,
        )[0]
        if d:
            parts[d] = send_tm(p, parts[d], d)

    def join(blocks, begins):
        shape = [sds((p.local, p.chans, p.rows, p.lon), F32)]
        held = [scratch((1, n, p.cp, p.out), F32)]
        return call(kernel(join_kernel, p, [begins]), shape, held, blocks, 8 << 20, 1, states=p.local, outs_by=True)[0]

    begins = [0, 0] + [p.out] * (n - 2)
    return join(scores[:2] + parts[2:], begins), join(parts, [0] * n)


def back_order(n):
    return [*range(n - 2, 1, -1), n - 1, 1, 0]


def solution(mesh):
    in_specs = (P("tm", None, "lat", None), P("tm", None, "lat", None), P(), P(), P(), P())
    out_specs = (P("tm", None, "lat", None), P("tm", None, "lat", None))
    return jax.shard_map(shards, mesh=mesh, in_specs=in_specs, out_specs=out_specs, check_vma=False)
```
